512 devices in a mesh: seq: 32 (over x, y), exp: 16 (over z, core).
Axes of the slice: x: 4, y: 8, z: 8, core: 2. Of those that a mesh axis runs over, the one named last changes fastest.
Arguments:
- mixer_query: bfloat16 [16, 2048, 1024], P('exp', 'seq'), may hold values from -6 to 6
- mixer_key: bfloat16 [16, 2048, 1024], P('exp', 'seq'), may hold values from -6 to 6
- mixer_value: bfloat16 [16, 2048, 2048], P('exp', 'seq'), may hold values from -6 to 6
- log_decay: bfloat16 [16, 2048, 16], P('exp', 'seq'), may hold values from -0.75 to 0
- strength: bfloat16 [16, 2048, 16], P('exp', 'seq'), may hold values from 0 to 0.9
- residual: bfloat16 [16, 2048, 2048], P('exp', 'seq'), may hold values from -6 to 6
- out_gain: float32 [128], replicated, may hold values from 0.25 to 1.75
- ffn_gain: float32 [2048], replicated, may hold values from 0.25 to 1.75
- expert_ids: int32 [16, 2048, 10], P('exp', 'seq'), may hold values from 0 to 511, all different within a row; in each aligned block of 64 rows (0 to 63, 64 to 127, ..., all dimensions but the last counted through in order) at most 2 rows name the same one
- expert_weights: float32 [16, 2048, 10], P('exp', 'seq'), may hold values from 0.05 to 0.25
- gate_proj: bfloat16 [512, 2048, 256], P(('seq', 'exp')), may hold values from -0.125 to 0.125
- up_proj: bfloat16 [512, 2048, 256], P(('seq', 'exp')), may hold values from -0.125 to 0.125
- down_proj: bfloat16 [512, 256, 2048], P(('seq', 'exp')), may hold values from -0.375 to 0.375
Outputs:
- mixed: bfloat16 [16, 2048, 2048], P('exp', 'seq')
- ffn_out: bfloat16 [16, 2048, 2048], P('exp', 'seq')
The draws below stay inside these ranges and needn't reach their ends.
Inputs may be any that keep to these rules, and one draw needn't show every extreme that they name: `expert_ids`: each row names 10 different experts; the 64 rows of one device (an aligned block) name no expert more than 2 times, and some block names an expert exactly 2 times.
All inputs are finite; a program needn't handle non-finite values.
Results may differ from the reference program's by a relative error of at most 0.018.
Values may be sent and summed in bfloat16 or wider, within the bound.
No kernel may reach another device: no remote copies, remote signals or barrier semaphores. Data moves between devices by JAX's collectives and lax.ppermute only.
A program may use at most 64 MiB of HBM per device.

```python
import math
import jax
import jax.numpy as jnp
import numpy as np
from jax import lax

D = 2048
DH = 128
HK = 8
VALUE_HEADS = 16
FFE = 256
TOPK = 10
BLOCK = 64
TOK_DEV = 64
SEGMENTS = 16
SEG_TOK = 2048
EXPERTS = 512
MOST = 2
DEVICES = 512


def gate_plan(key):
    base_key = jax.random.fold_in(key, 4099)
    layout_keys = jax.random.split(base_key, 6)
    head_order = jax.random.permutation(layout_keys[0], VALUE_HEADS)
    slow_count = VALUE_HEADS // 2
    gradual_head_count = head_order < slow_count
    gradual_decay_rate = jnp.exp(jax.random.uniform(layout_keys[1], (VALUE_HEADS,), jnp.float32, math.log(0.2), math.log(0.6)))
    quick_window = jnp.exp(jax.random.uniform(layout_keys[2], (VALUE_HEADS,), jnp.float32, math.log(30.0), math.log(50.0)))
    sequence_length = SEGMENTS * SEG_TOK
    spike_position = jax.random.randint(layout_keys[3], (3,), 0, sequence_length)
    spike_penalty = jax.random.uniform(layout_keys[4], (3, VALUE_HEADS), jnp.float32, 0.2, 0.5)
    block_scale_factor = jnp.exp(jax.random.uniform(layout_keys[5], (sequence_length // TOK_DEV, 1), jnp.float32, math.log(0.6), math.log(1.6)))
    return (gradual_head_count, gradual_decay_rate, quick_window, spike_position, spike_penalty, block_scale_factor)


def draw_log_decay(key, part):
    routing_layout = gate_plan(key)
    gradual_head_count = routing_layout[0]
    sequence_length = SEGMENTS * SEG_TOK
    roughness = jnp.exp(jax.random.uniform(jax.random.fold_in(key, 17), (sequence_length, VALUE_HEADS), jnp.float32, math.log(0.5), math.log(2.0)))
    factor = roughness * jnp.repeat(routing_layout[5], TOK_DEV, axis=0)
    slow_value = -routing_layout[1] * factor / sequence_length
    fast_value = -math.log(10.0) / routing_layout[2] * factor
    sampled_values = jnp.where(gradual_head_count, slow_value, fast_value)
    token_positions = jnp.arange(sequence_length)
    spike_component = jnp.sum(jnp.where(token_positions[:, None, None] == routing_layout[3][None, :, None], jnp.log(1.0 - routing_layout[4])[None, :, :], 0.0), axis=1)
    sampled_values = sampled_values + jnp.where(gradual_head_count, spike_component, 0.0)
    return sampled_values.reshape(SEGMENTS, SEG_TOK, VALUE_HEADS).astype(jnp.bfloat16)


def draw_strength(key, part):
    routing_layout = gate_plan(key)
    gradual_head_count = routing_layout[0]
    sequence_length = SEGMENTS * SEG_TOK
    roughness = jnp.exp(jax.random.uniform(jax.random.fold_in(key, 29), (sequence_length, VALUE_HEADS), jnp.float32, math.log(0.5), math.log(2.0)))
    slow_value = jnp.minimum(0.5 * DH / sequence_length * roughness * jnp.repeat(routing_layout[5], TOK_DEV, axis=0), 0.9)
    fast_value = jnp.exp(jax.random.uniform(jax.random.fold_in(key, 31), (sequence_length, VALUE_HEADS), jnp.float32, math.log(0.2), math.log(0.9)))
    sampled_values = jnp.where(gradual_head_count, slow_value, fast_value)
    return sampled_values.reshape(SEGMENTS, SEG_TOK, VALUE_HEADS).astype(jnp.bfloat16)


def steps_of(stream_key, shape, cuts, low, largest):
    def one(dim, shards_of):
        steps = jax.random.uniform(jax.random.fold_in(jax.random.fold_in(stream_key, 6), dim), (shards_of,), jnp.float32, low / len(cuts), largest / len(cuts))
        return jnp.repeat(jnp.exp(steps), shape[dim] // shards_of).reshape((-1,) + (1,) * (len(shape) - dim - 1))

    gain = one(*cuts[0])
    for cut in cuts[1:]:
        gain = gain * one(*cut)
    return gain


def deal_out(own_key, own, number, rows, number_of, top, bound, lean):
    ranking = jax.random.permutation(own_key, number_of)
    crowded, ordinary = load_shares(number_of, rows * top, bound, lean, True), load_shares(number_of, rows * top, bound, lean, False)
    places = jnp.arange(number_of)

    def named(lengths, offset_by):
        used = int((lengths > 0).sum())
        fixed = max(1, used // 4)
        moved = fixed + (places - fixed + offset_by * (used - fixed)) % max(1, number_of - fixed)
        return jnp.zeros((number_of,), jnp.int32).at[ranking[jnp.where(places < fixed, places, moved)]].set(jnp.asarray(lengths, jnp.int32))

    lengths = jnp.where(number % 4 == 0, named(crowded, number // 4), named(ordinary, number - number // 4 - 1))
    mixed = jax.random.permutation(jax.random.fold_in(own, 3), number_of)
    source_of, taker = mixed[0:number_of // 2 * 2:2], mixed[1:number_of // 2 * 2:2]
    margin = jnp.minimum(lengths[source_of] - 1, bound - lengths[taker]) // 2
    margin = jnp.where((source_of == ranking[0]) | (taker == ranking[0]) | (lengths[taker] == 0), 0, jnp.maximum(margin, 0))
    moved = jax.random.randint(jax.random.fold_in(own, 4), (number_of // 2,), 0, 1 << 20) % (margin + 1)
    lengths = lengths.at[source_of].add(-moved).at[taker].add(moved)
    labels = jnp.searchsorted(jnp.cumsum(lengths), jnp.arange(rows * top), side="right").astype(jnp.int32)
    listing = labels.reshape(top, rows).T
    listing = listing[jax.random.permutation(jax.random.fold_in(own, 1), rows)]
    offset_by = jax.random.randint(jax.random.fold_in(own, 2), (rows, 1), 0, top)
    return jnp.take_along_axis(listing, (jnp.arange(top)[None, :] + offset_by) % top, axis=1)


def load_shares(number_of, total, bound, skew, full):
    weights = [(1 << 20) // math.isqrt(rank ** skew) + 1 for rank in range(1, number_of + 1)]
    largest = bound if full else min(bound, max(-(-total // number_of), total * weights[0] // sum(weights)))
    least = 1 if total - largest >= number_of - 1 else 0
    given, rest = [largest] + [least] * (number_of - 1), total - largest - least * (number_of - 1)
    while rest > 0:
        movable = [i for i in range(1, number_of) if given[i] < largest] or [i for i in range(1, number_of) if given[i] < bound]
        whole, remaining = sum([weights[i] for i in movable]), rest
        for i in movable:
            more = min(bound - given[i], max(1, remaining * weights[i] // whole), rest)
            given[i] = given[i] + more
            rest = rest - more
    return np.array(given)


def bell_draw(rng, dims, scale, reach, cuts=(), kind=jnp.bfloat16):
    values = scale * jax.random.normal(rng, dims, jnp.float32)
    if cuts:
        values = values * steps_of(rng, dims, cuts, -0.22, 0.18)
    return jnp.clip(values, -reach, reach).astype(kind)


def setup_inputs(seed: int = 0) -> dict:
    splits = jax.random.split(jax.random.key(seed), 14)
    mixer_query = bell_draw(splits[0], (SEGMENTS, SEG_TOK, HK * DH), 1.0, 6.0, ((0, 16), (1, 32)))
    mixer_key = bell_draw(splits[1], (SEGMENTS, SEG_TOK, HK * DH), 1.0, 6.0, ((0, 16), (1, 32)))
    mixer_value = bell_draw(splits[2], (SEGMENTS, SEG_TOK, VALUE_HEADS * DH), 1.0, 6.0, ((0, 16), (1, 32)))
    log_decay = draw_log_decay(jax.random.fold_in(splits[13], 71), 0)
    strength = draw_strength(jax.random.fold_in(splits[13], 71), 0)
    residual = bell_draw(splits[5], (SEGMENTS, SEG_TOK, D), 1.0, 6.0, ((0, 16), (1, 32)))
    out_gain = jnp.clip(1.0 + 0.15 * jax.random.normal(splits[6], (DH,), jnp.float32), 0.25, 1.75)
    ffn_gain = jnp.clip(1.0 + 0.15 * jax.random.normal(splits[7], (D,), jnp.float32), 0.25, 1.75)
    expert_ids_keys = jax.random.split(jax.random.fold_in(splits[8], 1), SEGMENTS * SEG_TOK // TOK_DEV)
    expert_ids_turns = jax.random.permutation(jax.random.fold_in(splits[8], 3), SEGMENTS * SEG_TOK // TOK_DEV)
    expert_ids = jax.vmap(lambda own, number: deal_out(jax.random.fold_in(splits[8], 2), own, number, TOK_DEV, EXPERTS, TOPK, MOST, 2))(expert_ids_keys, expert_ids_turns).reshape((SEGMENTS, SEG_TOK, TOPK))
    expert_weights = jnp.clip(0.05 + 0.2 * jax.random.uniform(splits[9], (SEGMENTS, SEG_TOK, TOPK), jnp.float32) ** steps_of(splits[9], (SEGMENTS, SEG_TOK, TOPK), ((0, 16), (1, 32)), -0.2, 0.2), 0.05, 0.25)
    gate_proj = bell_draw(splits[10], (EXPERTS, D, FFE), D ** -0.5, 0.125, ((0, 512),))
    up_proj = bell_draw(splits[11], (EXPERTS, D, FFE), D ** -0.5, 0.125, ((0, 512),))
    down_proj = bell_draw(splits[12], (EXPERTS, FFE, D), FFE ** -0.5, 0.375, ((0, 512),))
    return {"mixer_query": mixer_query, "mixer_key": mixer_key, "mixer_value": mixer_value, "log_decay": log_decay, "strength": strength, "residual": residual, "out_gain": out_gain, "ffn_gain": ffn_gain, "expert_ids": expert_ids, "expert_weights": expert_weights, "gate_proj": gate_proj, "up_proj": up_proj, "down_proj": down_proj}


def unit_rows(matrix):
    matrix = matrix.astype(jnp.float32)
    return matrix * lax.rsqrt(lax.optimization_barrier(jnp.sum(matrix * matrix, axis=-1, keepdims=True)) + 1e-06)

def block_parts(query_rows, key_rows, values, decay_rows, strength_rows):
    block_size = query_rows.shape[1]
    cumulative = jnp.cumsum(decay_rows, axis=1)
    spread = cumulative[:, :, None] - cumulative[:, None, :]
    row_index = lax.broadcasted_iota(jnp.int32, (block_size, block_size), 0)
    col_index = lax.broadcasted_iota(jnp.int32, (block_size, block_size), 1)
    strict_lower = row_index > col_index
    inclusive = row_index >= col_index
    fade_lower = jnp.where(strict_lower, jnp.exp(jnp.where(strict_lower, spread, 0.0)), 0.0)
    fade_inclusive = jnp.where(inclusive, jnp.exp(jnp.where(inclusive, spread, 0.0)), 0.0)
    key_dot = jnp.einsum('nik,njk->nij', key_rows, key_rows, precision=lax.Precision.HIGHEST)
    query_dot = jnp.einsum('nik,njk->nij', query_rows, key_rows, precision=lax.Precision.HIGHEST)
    negated = -(strength_rows[:, :, None] * key_dot * fade_lower)
    identity_block = jnp.eye(block_size, dtype=jnp.float32)
    inverse = identity_block + negated
    powered = negated
    for level_index in range(block_size.bit_length() - 2):
        powered = jnp.einsum('nij,njk->nik', powered, powered, precision=lax.Precision.HIGHEST)
        inverse = jnp.einsum('nij,njk->nik', inverse, identity_block + powered, precision=lax.Precision.HIGHEST)
    decay_gain = jnp.exp(cumulative)
    last_total = cumulative[:, -1:]
    tail_gain = jnp.exp(last_total - cumulative)
    beta_keys = (strength_rows * decay_gain)[:, :, None] * key_rows
    weighted_keys = jnp.einsum('nij,njk->nik', inverse, beta_keys, precision=lax.Precision.HIGHEST)
    updated_value_rows = jnp.einsum('nij,njk->nik', inverse, strength_rows[:, :, None] * values, precision=lax.Precision.HIGHEST)
    scores = query_dot * fade_inclusive
    query_part = decay_gain[:, :, None] * query_rows - jnp.einsum('nij,njk->nik', scores, weighted_keys, precision=lax.Precision.HIGHEST)
    local_out = jnp.einsum('nij,njk->nik', scores, updated_value_rows, precision=lax.Precision.HIGHEST)
    attenuated_keys = tail_gain[:, :, None] * key_rows
    key_identity = jnp.eye(key_rows.shape[2], dtype=jnp.float32)
    transition = jnp.exp(last_total)[:, :, None] * key_identity - jnp.einsum('nck,ncl->nkl', attenuated_keys, weighted_keys, precision=lax.Precision.HIGHEST)
    inserted_signal = jnp.einsum('wjf,wjd->wfd', attenuated_keys, updated_value_rows, precision=lax.Precision.HIGHEST)
    return (query_part, local_out, transition, inserted_signal)

def reference(mixer_query, mixer_key, mixer_value, log_decay, strength, residual, out_gain, ffn_gain, expert_ids, expert_weights, gate_proj, up_proj, down_proj):
    total = SEGMENTS * SEG_TOK
    block_count = total // BLOCK
    queries = mixer_query.reshape(total, HK, DH)
    keys_all = mixer_key.reshape(total, HK, DH)
    values_all = mixer_value.reshape(total, VALUE_HEADS, DH)
    decay_all = log_decay.reshape(total, VALUE_HEADS).astype(jnp.float32)
    strength_all = strength.reshape(total, VALUE_HEADS).astype(jnp.float32)
    ratio = VALUE_HEADS // HK

    def one_head(head):
        key_head = head // ratio
        query_rows = unit_rows(lax.dynamic_index_in_dim(queries, key_head, 1, keepdims=False))
        key_rows = unit_rows(lax.dynamic_index_in_dim(keys_all, key_head, 1, keepdims=False))
        value_rows = lax.dynamic_index_in_dim(values_all, head, 1, keepdims=False).astype(jnp.float32)
        decay_rows = lax.dynamic_index_in_dim(decay_all, head, 1, keepdims=False)
        strength_rows = lax.dynamic_index_in_dim(strength_all, head, 1, keepdims=False)
        parts = block_parts(query_rows.reshape(block_count, BLOCK, DH), key_rows.reshape(block_count, BLOCK, DH), value_rows.reshape(block_count, BLOCK, DH), decay_rows.reshape(block_count, BLOCK), strength_rows.reshape(block_count, BLOCK))

        def advance(carried, pieces):
            query_part, local_out, transition, inserted_signal = pieces
            emitted = jnp.dot(query_part, carried, precision=lax.Precision.HIGHEST) + local_out
            return (jnp.dot(transition, carried, precision=lax.Precision.HIGHEST) + inserted_signal, emitted)
        start_state = jnp.zeros((DH, DH), jnp.float32)
        final_state, emitted_all = lax.scan(advance, start_state, parts)
        return emitted_all.reshape(total, DH)
    head_out = lax.map(one_head, jnp.arange(VALUE_HEADS, dtype=jnp.int32))
    head_round = lax.optimization_barrier(jnp.transpose(head_out, (1, 0, 2)).astype(jnp.bfloat16)).astype(jnp.float32)
    normed = head_round * lax.rsqrt(lax.optimization_barrier(jnp.mean(head_round * head_round, axis=-1, keepdims=True)) + 1e-06) * out_gain
    mixed = (residual.reshape(total, D).astype(jnp.float32) + normed.reshape(total, D)).astype(jnp.bfloat16)
    mixed_wide = lax.optimization_barrier(mixed).astype(jnp.float32)
    ffn_in = (mixed_wide * lax.rsqrt(lax.optimization_barrier(jnp.mean(mixed_wide * mixed_wide, axis=-1, keepdims=True)) + 1e-06) * ffn_gain).astype(jnp.bfloat16)
    assign_count = total * TOPK
    flat_ids = expert_ids.reshape(assign_count).astype(jnp.int32)
    token_of = (jnp.arange(assign_count, dtype=jnp.int32) // TOPK).astype(jnp.int32)
    sort_order = jnp.argsort(flat_ids, stable=True)
    sorted_ids = flat_ids[sort_order]
    sorted_tokens = token_of[sort_order]
    sorted_weights = expert_weights.reshape(assign_count).astype(jnp.float32)[sort_order]
    expert_range = jnp.arange(EXPERTS, dtype=jnp.int32)
    run_start = jnp.searchsorted(sorted_ids, expert_range, side='left').astype(jnp.int32)
    run_length = (jnp.searchsorted(sorted_ids, expert_range + 1, side='left').astype(jnp.int32) - run_start).astype(jnp.int32)
    capacity = DEVICES * MOST
    slot_range = jnp.arange(capacity, dtype=jnp.int32)

    def one_expert(running, expert):
        live_slot = slot_range < run_length[expert]
        picked = jnp.clip(run_start[expert] + slot_range, 0, assign_count - 1).astype(jnp.int32)
        token_index = sorted_tokens[picked]
        row_block = ffn_in[token_index]
        gate_value = jnp.dot(row_block, gate_proj[expert], preferred_element_type=jnp.float32)
        up_value = jnp.dot(row_block, up_proj[expert], preferred_element_type=jnp.float32)
        hidden = (jax.nn.silu(gate_value) * up_value).astype(jnp.bfloat16)
        result = lax.optimization_barrier(jnp.dot(hidden, down_proj[expert], preferred_element_type=jnp.float32).astype(jnp.bfloat16)).astype(jnp.float32)
        slot_weight = jnp.where(live_slot, sorted_weights[picked], 0.0)
        return (running.at[token_index].add(slot_weight[:, None] * result), None)
    running, unused = lax.scan(one_expert, jnp.zeros((total, D), jnp.float32), expert_range)
    ffn_out = running.astype(jnp.bfloat16)
    return (mixed.reshape(SEGMENTS, SEG_TOK, D), ffn_out.reshape(SEGMENTS, SEG_TOK, D))
```

```python
import jax
import jax.numpy as jnp
from jax import lax
from jax.experimental import pallas as pl
from jax.experimental.pallas import tpu as pltpu
from jax.sharding import PartitionSpec as P

D = 2048
DH = 128
HK = 8
VALUE_HEADS = 16
TOPK = 10
BLOCK = 64
TOK = 64
EXPERTS = 512
LANES = 32
WIDTH = 64
BLOCKS = 32
CHUNKS = 4
STEPS = 8
SEGMENTS = 16
MAP_ROWS = DH + WIDTH
SLOTS = 2 * EXPERTS
COLS = D // 128
F32 = jnp.float32
BF16 = jnp.bfloat16
VMEM_LIMIT = 56 * 1024 * 1024


def params():
    return pltpu.CompilerParams(vmem_limit_bytes=VMEM_LIMIT)


def full(*arrays):
    return [pl.BlockSpec(memory_space=pltpu.VMEM) for _ in arrays]


def dot_nn(a, b):
    return lax.dot_general(a, b, (((1,), (0,)), ((), ())), preferred_element_type=F32)


def dot_nt(a, b):
    return lax.dot_general(a, b, (((1,), (1,)), ((), ())), preferred_element_type=F32)


def bdot_nn(a, b):
    return lax.dot_general(a, b, (((2,), (1,)), ((0,), (0,))), preferred_element_type=F32)


def bdot_nt(a, b):
    return lax.dot_general(a, b, (((2,), (2,)), ((0,), (0,))), preferred_element_type=F32)


def split(x):
    high = x.astype(BF16)
    return high, (x - high.astype(F32)).astype(BF16)


def bdot3(a, b):
    ah, al = split(a)
    bh, bl = split(b)
    return bdot_nn(ah, bh) + (bdot_nn(ah, bl) + bdot_nn(al, bh))


def swap_matrix():
    out_index = lax.broadcasted_iota(jnp.int32, (256, 256), 0)
    in_index = lax.broadcasted_iota(jnp.int32, (256, 256), 1)
    return (in_index == (out_index % 16) * 16 + out_index // 16).astype(BF16)


def pack_kernel(query_ref, key_ref, value_ref, decay_ref, strength_ref, out_ref):
    lane = lax.broadcasted_iota(jnp.int32, (TOK, 128), 1)
    for index in range(LANES):
        key_head, head, half = index // 4, index // 2, index % 2
        out_ref[index, 0:64, :] = query_ref[:, key_head * 128 : key_head * 128 + 128]
        out_ref[index, 64:128, :] = key_ref[:, key_head * 128 : key_head * 128 + 128]
        piece = value_ref[:, head * 128 : head * 128 + 128].astype(F32)
        if half:
            piece = pltpu.roll(piece, 64, 1)
        decay = jnp.broadcast_to(decay_ref[:, head : head + 1].astype(F32), (TOK, 128))
        strength = jnp.broadcast_to(strength_ref[:, head : head + 1].astype(F32), (TOK, 128))
        piece = jnp.where(lane < 64, piece, jnp.where(lane == 64, decay, strength))
        out_ref[index, 128:192, :] = piece.astype(BF16)


def route_kernel(ids_ref, tok_ref, slot_ref):
    expert = lax.broadcasted_iota(jnp.int32, (TOK, EXPERTS), 1)
    named = jnp.zeros((TOK, EXPERTS), F32)
    for k in range(TOPK):
        named = jnp.where(ids_ref[:, k : k + 1] == expert, 1.0, named)
    row = lax.broadcasted_iota(jnp.int32, (TOK, TOK), 0)
    col = lax.broadcasted_iota(jnp.int32, (TOK, TOK), 1)
    rank = dot_nn((row > col).astype(BF16), named.astype(BF16))
    token = lax.broadcasted_iota(jnp.int32, (TOK, EXPERTS), 0).astype(F32)
    first = jnp.sum(jnp.where(rank == 0.0, token * named, 0.0), axis=0, keepdims=True)
    second = jnp.sum(jnp.where(rank == 1.0, token * named, 0.0), axis=0, keepdims=True)
    tok_ref[...] = jnp.concatenate([first, second], axis=0).astype(jnp.int32)
    lane = lax.broadcasted_iota(jnp.int32, (TOK, 128), 1)
    slots = jnp.zeros((TOK, 128), jnp.int32)
    for k in range(TOPK):
        ids = ids_ref[:, k : k + 1]
        mine = jnp.sum(jnp.where(ids == expert, rank, 0.0), axis=1, keepdims=True)
        slots = jnp.where(lane == k, 2 * ids + mine.astype(jnp.int32), slots)
    slot_ref[...] = slots


def mixer_kernel(
    recv_ref,
    query_part_ref,
    local_ref,
    sub_map_ref,
    sub_gain_ref,
    send_ref,
    w_ref,
    u_ref,
    k_ref,
    gain_ref,
):
    row = lax.broadcasted_iota(jnp.int32, (BLOCK, BLOCK), 0)
    col = lax.broadcasted_iota(jnp.int32, (BLOCK, BLOCK), 1)
    eye = (row == col)[None]
    inclusive = (row >= col)[None]
    upper = (row <= col)[None]
    lower = (row > col)[None]
    group = STEPS

    def same(size):
        return ((row // size) == (col // size))[None]

    identity = jnp.broadcast_to(eye.astype(F32), (group, BLOCK, BLOCK))
    identity_half = identity.astype(BF16)

    def parts(step, unused):
        start = step * group
        block = recv_ref[pl.ds(start, group)]
        q = block[:, 0:64]
        k = block[:, 64:128]
        extra = block[:, 128:192]
        qf = q.astype(F32)
        kf = k.astype(F32)
        q_norm = lax.rsqrt(jnp.sum(qf * qf, axis=2, keepdims=True) + 1e-06)
        k_norm = lax.rsqrt(jnp.sum(kf * kf, axis=2, keepdims=True) + 1e-06)
        k_norm_row = jnp.sum(jnp.where(eye, k_norm, 0.0), axis=1, keepdims=True)
        decay = extra[:, :, 64:65].astype(F32)
        strength = extra[:, :, 65:66].astype(F32)
        strength_row = jnp.sum(jnp.where(eye, strength, 0.0), axis=1, keepdims=True)
        decay_row = jnp.sum(jnp.where(eye, decay, 0.0), axis=1, keepdims=True)
        cum_row = jnp.sum(jnp.where(upper, decay, 0.0), axis=1, keepdims=True)
        cum = jnp.sum(jnp.where(inclusive, decay_row, 0.0), axis=2, keepdims=True)
        spread = cum - cum_row
        fade = jnp.where(inclusive, jnp.exp(jnp.where(inclusive, spread, 0.0)), 0.0)
        key_dot = bdot_nt(k, k) * (k_norm * k_norm_row)
        query_dot = bdot_nt(q, k) * (q_norm * k_norm_row)
        negated = jnp.where(lower, -(strength * key_dot * fade), 0.0)
        base = jnp.where(same(8), negated, 0.0)
        inverse = identity + base
        powered = bdot3(base, base)
        inverse = inverse + bdot3(inverse, powered)
        powered = bdot3(powered, powered)
        inverse = inverse + bdot3(inverse, powered)
        for size in (8, 16, 32):
            cross = jnp.where(same(2 * size) & ~same(size), negated, 0.0).astype(BF16)
            half = inverse.astype(BF16)
            inverse = inverse + bdot_nn(bdot_nn(half, cross).astype(BF16), half)
        inverse_half = inverse.astype(BF16)
        decay_gain = jnp.exp(cum)
        last = cum[:, BLOCK - 1 : BLOCK, :]
        tail = jnp.exp(last - cum)
        unit_k = k_norm * kf
        w = bdot_nn(inverse_half, ((strength * decay_gain) * unit_k).astype(BF16)).astype(BF16)
        v_t = bdot_nt(identity_half, extra[:, :, 0:64]) * strength_row
        u_t = bdot_nt(v_t.astype(BF16), inverse_half)
        scores = (query_dot * fade).astype(BF16)
        q_part = decay_gain * (q_norm * qf) - bdot_nn(scores, w)
        local = bdot_nt(scores, u_t.astype(BF16))
        w_ref[pl.ds(start, group)] = w
        u_ref[pl.ds(start, group)] = u_t
        k_ref[pl.ds(start, group)] = (tail * unit_k).astype(BF16)
        gain_ref[pl.ds(start, group)] = jnp.broadcast_to(jnp.exp(last), (group, 8, 128))
        query_part_ref[pl.ds(start, group)] = q_part.astype(BF16)
        local_ref[pl.ds(start, group)] = local
        return unused

    lax.fori_loop(0, BLOCKS // group, parts, 0)

    map_row = lax.broadcasted_iota(jnp.int32, (MAP_ROWS, DH), 0)
    map_col = lax.broadcasted_iota(jnp.int32, (MAP_ROWS, DH), 1)
    diagonal = map_row == map_col
    start_map = jnp.where(diagonal, 1.0, 0.0).astype(F32)

    def advance(step, carried):
        maps, gains = carried
        new_maps, new_gains = [], []
        for chunk in range(CHUNKS):
            index = chunk * STEPS + step
            state = maps[chunk]
            half = state.astype(BF16)
            out = dot_nt(query_part_ref[index], half)
            seen = dot_nt(half, w_ref[index])
            fresh = jnp.concatenate([-seen[0:DH], u_ref[index] - seen[DH:MAP_ROWS]], axis=0)
            gain = gain_ref[index][0:1, :]
            query_part_ref[index] = out[:, 0:DH].astype(BF16)
            local_ref[index] = local_ref[index] + out[:, DH:MAP_ROWS]
            new_maps.append(gain * state + dot_nn(fresh.astype(BF16), k_ref[index]))
            new_gains.append(gain * gains[chunk])
        return tuple(new_maps), tuple(new_gains)

    maps, gains = lax.fori_loop(
        0,
        STEPS,
        advance,
        (
            tuple(start_map for _ in range(CHUNKS)),
            tuple(jnp.ones((1, DH), F32) for _ in range(CHUNKS)),
        ),
    )
    whole = None
    for chunk in range(CHUNKS):
        gain = gains[chunk]
        changed = maps[chunk] - jnp.where(diagonal, gain, 0.0)
        sub_map_ref[chunk] = changed
        sub_gain_ref[chunk] = jnp.broadcast_to(gain, (8, DH))
        if whole is None:
            whole, total = maps[chunk], gain
        else:
            added = jnp.where(map_row < DH, 0.0, changed)
            whole = gain * whole + dot_nn(whole.astype(BF16), changed[0:DH].astype(BF16)) + added
            total = gain * total
    send_ref[0:MAP_ROWS, :] = (whole - jnp.where(diagonal, total, 0.0)).astype(BF16)
    high, low = split(total)
    send_ref[MAP_ROWS : MAP_ROWS + 16, :] = jnp.broadcast_to(high.astype(F32), (16, DH)).astype(BF16)
    send_ref[MAP_ROWS + 16 : MAP_ROWS + 32, :] = jnp.broadcast_to(low.astype(F32), (16, DH)).astype(BF16)


def fold_kernel(
    position_ref, maps_ref, query_part_ref, local_ref, sub_map_ref, sub_gain_ref, out_ref
):
    def fold(index, state):
        gain = (
            maps_ref[index, MAP_ROWS : MAP_ROWS + 16, :].astype(F32)
            + maps_ref[index, MAP_ROWS + 16 : MAP_ROWS + 32, :].astype(F32)
        )[0:1]
        return (
            gain * state
            + dot_nn(state.astype(BF16), maps_ref[index, 0:DH, :])
            + maps_ref[index, DH:MAP_ROWS, :].astype(F32)
        )

    state = lax.fori_loop(0, position_ref[0], fold, jnp.zeros((WIDTH, DH), F32))
    for chunk in range(CHUNKS):
        half = state.astype(BF16)
        for step in range(STEPS):
            index = chunk * STEPS + step
            out = dot_nt(query_part_ref[index], half) + local_ref[index]
            out_ref[index] = jnp.concatenate([out[0:32], out[32:64]], axis=1).astype(BF16)
        if chunk + 1 < CHUNKS:
            changed = sub_map_ref[chunk]
            state = (
                sub_gain_ref[chunk][0:1] * state
                + dot_nn(half, changed[0:DH].astype(BF16))
                + changed[DH:MAP_ROWS]
            )


def mixed_kernel(
    tok_ref, heads_ref, residual_ref, out_gain_ref, ffn_gain_ref, mixed_ref, send_ref, rows_ref
):
    lane = lax.broadcasted_iota(jnp.int32, (32, 128), 1)
    gain = out_gain_ref[...]
    total = jnp.zeros((TOK, 1), F32)
    for head in range(VALUE_HEADS):
        left = heads_ref[2 * head].astype(F32)
        right = heads_ref[2 * head + 1].astype(F32)
        top = jnp.where(lane < 64, left, pltpu.roll(right, 64, 1))
        bottom = jnp.where(lane < 64, pltpu.roll(left, 64, 1), right)
        wide = jnp.concatenate([top, bottom], axis=0)
        scale = lax.rsqrt(jnp.mean(wide * wide, axis=1, keepdims=True) + 1e-06)
        part = slice(head * DH, head * DH + DH)
        mixed = (residual_ref[:, part].astype(F32) + wide * scale * gain).astype(BF16)
        mixed_ref[:, part] = mixed
        mixed_wide = mixed.astype(F32)
        total = total + jnp.sum(mixed_wide * mixed_wide, axis=1, keepdims=True)
    scale = lax.rsqrt(total * (1.0 / D) + 1e-06)
    swap = swap_matrix()
    for group in range(TOK // 16):
        tokens = slice(group * 16, group * 16 + 16)
        pieces = []
        for c in range(COLS):
            part = slice(c * 128, c * 128 + 128)
            value = mixed_ref[tokens, part].astype(F32) * scale[tokens] * ffn_gain_ref[:, part]
            pieces.append(value.astype(BF16))
        swapped = dot_nn(swap, jnp.concatenate(pieces, axis=0)).astype(BF16)
        rows_ref[tokens] = swapped.reshape(16, 16, 128)

    def place(expert, unused):
        send_ref[2 * expert] = rows_ref[tok_ref[0, expert]]
        send_ref[2 * expert + 1] = rows_ref[tok_ref[1, expert]]
        return unused

    lax.fori_loop(0, EXPERTS, place, 0, unroll=16)


FFN_ROWS = 256


def expert_kernel(rows_ref, gate_ref, up_ref, down_ref, out_ref, wide_ref):
    swap = swap_matrix()
    for group in range(FFN_ROWS // 16):
        tile = dot_nn(swap, rows_ref[group * 256 : group * 256 + 256, :]).astype(BF16)
        for c in range(COLS):
            wide_ref[group * 16 : group * 16 + 16, c * 128 : c * 128 + 128] = tile[
                c * 16 : c * 16 + 16
            ]
    wide = wide_ref[...]
    gate = dot_nn(wide, gate_ref[...])
    up = dot_nn(wide, up_ref[...])
    hidden = (gate / (1.0 + jnp.exp(-gate)) * up).astype(BF16)
    wide_ref[...] = dot_nn(hidden, down_ref[...]).astype(BF16)
    for group in range(FFN_ROWS // 16):
        pieces = [
            wide_ref[group * 16 : group * 16 + 16, c * 128 : c * 128 + 128] for c in range(COLS)
        ]
        out_ref[group * 256 : group * 256 + 256, :] = dot_nn(
            swap, jnp.concatenate(pieces, axis=0)
        ).astype(BF16)


def combine_kernel(slot_ref, weight_ref, rows_ref, out_ref, sum_ref):
    def token(index, unused):
        total = jnp.zeros((16, 128), F32)
        for k in range(TOPK):
            total = total + weight_ref[index, k] * rows_ref[slot_ref[index, k]].astype(F32)
        sum_ref[index] = total.astype(BF16)
        return unused

    lax.fori_loop(0, TOK, token, 0, unroll=2)
    swap = swap_matrix()
    for group in range(TOK // 16):
        tokens = slice(group * 16, group * 16 + 16)
        tile = dot_nn(swap, sum_ref[tokens].reshape(256, 128)).astype(BF16)
        for c in range(COLS):
            out_ref[tokens, c * 128 : c * 128 + 128] = tile[c * 16 : c * 16 + 16]


def shape(dims, dtype):
    return jax.ShapeDtypeStruct(dims, dtype)


SMEM = pl.BlockSpec(memory_space=pltpu.SMEM)
WHOLE = pl.BlockSpec(memory_space=pltpu.VMEM)


def pack(query, key, value, decay, strength):
    return pl.pallas_call(
        pack_kernel,
        out_shape=shape((LANES, 192, 128), BF16),
        in_specs=[WHOLE] * 5,
        out_specs=WHOLE,
        compiler_params=params(),
        name="pack",
    )(query, key, value, decay, strength)


def route(ids):
    return pl.pallas_call(
        route_kernel,
        out_shape=(shape((2, EXPERTS), jnp.int32), shape((TOK, 128), jnp.int32)),
        in_specs=[WHOLE],
        out_specs=(WHOLE, WHOLE),
        compiler_params=params(),
        name="route",
    )(ids)


def mixer(received):
    return pl.pallas_call(
        mixer_kernel,
        out_shape=(
            shape((BLOCKS, BLOCK, DH), BF16),
            shape((BLOCKS, BLOCK, WIDTH), F32),
            shape((CHUNKS, MAP_ROWS, DH), F32),
            shape((CHUNKS, 8, DH), F32),
            shape((MAP_ROWS + 32, DH), BF16),
        ),
        in_specs=[WHOLE],
        out_specs=(WHOLE,) * 5,
        scratch_shapes=[
            pltpu.VMEM((BLOCKS, BLOCK, DH), BF16),
            pltpu.VMEM((BLOCKS, WIDTH, BLOCK), F32),
            pltpu.VMEM((BLOCKS, BLOCK, DH), BF16),
            pltpu.VMEM((BLOCKS, 8, DH), F32),
        ],
        compiler_params=params(),
        name="mixer",
    )(received)


def fold(position, maps, query_part, local, sub_map, sub_gain):
    return pl.pallas_call(
        fold_kernel,
        out_shape=shape((BLOCKS, 32, 128), BF16),
        in_specs=[SMEM] + [WHOLE] * 5,
        out_specs=WHOLE,
        compiler_params=params(),
        name="fold",
    )(position, maps, query_part, local, sub_map, sub_gain)


def mix(tok, heads, residual, out_gain, ffn_gain):
    return pl.pallas_call(
        mixed_kernel,
        out_shape=(shape((TOK, D), BF16), shape((SLOTS, 16, 128), BF16)),
        in_specs=[SMEM] + [WHOLE] * 4,
        out_specs=(WHOLE, WHOLE),
        scratch_shapes=[pltpu.VMEM((TOK, 16, 128), BF16)],
        compiler_params=params(),
        name="mix",
    )(tok, heads, residual, out_gain, ffn_gain)


def experts(rows, gate, up, down):
    hidden = gate.shape[1]
    block = pl.BlockSpec((FFN_ROWS * 16, 128), lambda i: (i, 0))
    return pl.pallas_call(
        expert_kernel,
        grid=(SLOTS // FFN_ROWS,),
        out_shape=shape((SLOTS * 16, 128), BF16),
        in_specs=[
            block,
            pl.BlockSpec((D, hidden), lambda i: (0, 0)),
            pl.BlockSpec((D, hidden), lambda i: (0, 0)),
            pl.BlockSpec((hidden, D), lambda i: (0, 0)),
        ],
        out_specs=block,
        scratch_shapes=[pltpu.VMEM((FFN_ROWS, D), BF16)],
        compiler_params=params(),
        name="experts",
    )(rows, gate, up, down)


def combine(slots, weights, rows):
    return pl.pallas_call(
        combine_kernel,
        out_shape=shape((TOK, D), BF16),
        in_specs=[SMEM, SMEM, WHOLE],
        out_specs=WHOLE,
        scratch_shapes=[pltpu.VMEM((TOK, 16, 128), BF16)],
        compiler_params=params(),
        name="combine",
    )(slots, weights, rows)


def swap_all(x, axes):
    return lax.all_to_all(x, axes, split_axis=0, concat_axis=0, tiled=True)


def body(
    mixer_query,
    mixer_key,
    mixer_value,
    log_decay,
    strength,
    residual,
    out_gain,
    ffn_gain,
    expert_ids,
    expert_weights,
    gate_proj,
    up_proj,
    down_proj,
):
    sent = pack(mixer_query[0], mixer_key[0], mixer_value[0], log_decay[0], strength[0])
    received = swap_all(sent, "seq")
    tok, slots = route(expert_ids[0])
    query_part, local, sub_map, sub_gain, own_map = mixer(received)
    maps = lax.all_gather(own_map, "exp", axis=0)
    position = lax.axis_index("exp").astype(jnp.int32).reshape(1)
    head_rows = fold(position, maps, query_part, local, sub_map, sub_gain)
    heads = swap_all(head_rows, "seq")
    mixed, outgoing = mix(
        tok, heads, residual[0], out_gain.reshape(1, DH), ffn_gain.reshape(1, D)
    )
    arrived = swap_all(outgoing, ("seq", "exp"))
    result = experts(arrived.reshape(SLOTS * 16, 128), gate_proj[0], up_proj[0], down_proj[0])
    returned = swap_all(result.reshape(SLOTS, 16, 128), ("seq", "exp"))
    ffn_out = combine(slots, expert_weights[0], returned)
    return (mixed[None], ffn_out[None])


def solution(mesh):
    rows = P("exp", "seq", None)
    owned = P(("seq", "exp"), None, None)
    return jax.shard_map(
        body,
        mesh=mesh,
        in_specs=(rows,) * 6 + (P(), P(), rows, rows) + (owned,) * 3,
        out_specs=(rows, rows),
        check_vma=False,
    )
```

```python
import jax
import jax.numpy as jnp
from jax import lax
from jax.experimental import pallas as pl
from jax.experimental.pallas import tpu as pltpu
from jax.sharding import Mesh
from jax.sharding import PartitionSpec as P

D = 2048
DH = 128
HK = 8
VALUE_HEADS = 16
TOPK = 10
BLOCK = 64
TOK = 64
EXPERTS = 512
WIDTH = 64
BLOCKS = 16
GROUP = 8
CHUNKS = 4
STEPS = 4
PACK_ROWS = 3 * TOK + 16
MAP_ROWS = 2 * DH
HALF_ROWS = MAP_ROWS + 32
SEG_ROWS = DH + WIDTH + 32
SLOTS = 2 * EXPERTS
COLS = D // 128
F32 = jnp.float32
BF16 = jnp.bfloat16
VMEM_LIMIT = 28 * 1024 * 1024


def params():
    return pltpu.CompilerParams(vmem_limit_bytes=VMEM_LIMIT)


def full(*arrays):
    return [pl.BlockSpec(memory_space=pltpu.VMEM) for _ in arrays]


def dot_nn(a, b):
    return lax.dot_general(a, b, (((1,), (0,)), ((), ())), preferred_element_type=F32)


def dot_nt(a, b):
    return lax.dot_general(a, b, (((1,), (1,)), ((), ())), preferred_element_type=F32)


def bdot_nn(a, b):
    return lax.dot_general(a, b, (((2,), (1,)), ((0,), (0,))), preferred_element_type=F32)


def bdot_nt(a, b):
    return lax.dot_general(a, b, (((2,), (2,)), ((0,), (0,))), preferred_element_type=F32)


def split(x):
    high = x.astype(BF16)
    return high, (x - high.astype(F32)).astype(BF16)


def bdot3(a, b):
    ah, al = split(a)
    bh, bl = split(b)
    return bdot_nn(ah, bh) + (bdot_nn(ah, bl) + bdot_nn(al, bh))


def swap_matrix():
    out_index = lax.broadcasted_iota(jnp.int32, (256, 256), 0)
    in_index = lax.broadcasted_iota(jnp.int32, (256, 256), 1)
    return (in_index == (out_index % 16) * 16 + out_index // 16).astype(BF16)


def pack_kernel(query_ref, key_ref, value_ref, decay_ref, strength_ref, out_ref):
    gates = jnp.concatenate([decay_ref[...].astype(F32), strength_ref[...].astype(F32)], axis=1)
    for head in range(VALUE_HEADS):
        shared = slice(head // 2 * DH, head // 2 * DH + DH)
        out_ref[head, 0:64, :] = query_ref[:, shared]
        out_ref[head, 64:128, :] = key_ref[:, shared]
        out_ref[head, 128:192, :] = value_ref[:, head * DH : head * DH + DH]
        out_ref[head, 192:208, :] = jnp.broadcast_to(gates[head : head + 1], (16, 128)).astype(BF16)


def route_kernel(ids_ref, weight_in_ref, tok_ref, slot_ref, weight_ref):
    expert = lax.broadcasted_iota(jnp.int32, (TOK, EXPERTS), 1)
    named = jnp.zeros((TOK, EXPERTS), F32)
    for k in range(TOPK):
        named = jnp.where(ids_ref[:, k : k + 1] == expert, 1.0, named)
    row = lax.broadcasted_iota(jnp.int32, (TOK, TOK), 0)
    col = lax.broadcasted_iota(jnp.int32, (TOK, TOK), 1)
    rank = dot_nn((row > col).astype(BF16), named.astype(BF16))
    token = lax.broadcasted_iota(jnp.int32, (TOK, EXPERTS), 0).astype(F32)
    first = jnp.sum(jnp.where(rank == 0.0, token * named, 0.0), axis=0, keepdims=True)
    second = jnp.sum(jnp.where(rank == 1.0, token * named, 0.0), axis=0, keepdims=True)
    tok_ref[...] = jnp.concatenate([first, second], axis=0).astype(jnp.int32)
    lane = lax.broadcasted_iota(jnp.int32, (TOK, 128), 1)
    slots = jnp.zeros((TOK, 128), jnp.int32)
    weights = jnp.zeros((TOK, 128), F32)
    for k in range(TOPK):
        ids = ids_ref[:, k : k + 1]
        mine = jnp.sum(jnp.where(ids == expert, rank, 0.0), axis=1, keepdims=True)
        slots = jnp.where(lane == k, 2 * ids + mine.astype(jnp.int32), slots)
        weights = jnp.where(lane == k, weight_in_ref[:, k : k + 1], weights)
    slot_ref[...] = slots
    weight_ref[...] = weights


def spread_gain(gain):
    high, low = split(gain)
    rows = (16, DH)
    return (
        jnp.broadcast_to(high.astype(F32), rows).astype(BF16),
        jnp.broadcast_to(low.astype(F32), rows).astype(BF16),
    )


def read_gain(high, low):
    return (high.astype(F32) + low.astype(F32))[0:1]


def mixer_kernel(
    recv_ref,
    query_part_ref,
    local_ref,
    sub_map_ref,
    sub_gain_ref,
    send_ref,
    w_ref,
    u_ref,
    k_ref,
    gain_ref,
):
    row = lax.broadcasted_iota(jnp.int32, (BLOCK, BLOCK), 0)
    col = lax.broadcasted_iota(jnp.int32, (BLOCK, BLOCK), 1)
    eye = (row == col)[None]
    inclusive = (row >= col)[None]
    upper = (row <= col)[None]
    lower = (row > col)[None]

    def same(size):
        return ((row // size) == (col // size))[None]

    identity = jnp.broadcast_to(eye.astype(F32), (GROUP, BLOCK, BLOCK))
    wide_row = lax.broadcasted_iota(jnp.int32, (DH, DH), 0)
    wide_col = lax.broadcasted_iota(jnp.int32, (DH, DH), 1)
    wide_eye = jnp.broadcast_to((wide_row == wide_col).astype(F32)[None], (GROUP, DH, DH)).astype(BF16)

    def parts(step, unused):
        start = step * GROUP
        block = recv_ref[pl.ds(start, GROUP)]
        q = block[:, 0:64]
        k = block[:, 64:128]
        v = block[:, 128:192]
        gates = block[:, 192:208].astype(F32)
        decay_row = gates[:, 0:1, 0:64]
        strength_row = gates[:, 0:1, 64:128]
        qf = q.astype(F32)
        kf = k.astype(F32)
        q_norm = lax.rsqrt(jnp.sum(qf * qf, axis=2, keepdims=True) + 1e-06)
        k_norm = lax.rsqrt(jnp.sum(kf * kf, axis=2, keepdims=True) + 1e-06)
        k_norm_row = jnp.sum(jnp.where(eye, k_norm, 0.0), axis=1, keepdims=True)
        decay = jnp.sum(jnp.where(eye, decay_row, 0.0), axis=2, keepdims=True)
        strength = jnp.sum(jnp.where(eye, strength_row, 0.0), axis=2, keepdims=True)
        cum_row = jnp.sum(jnp.where(upper, decay, 0.0), axis=1, keepdims=True)
        cum = jnp.sum(jnp.where(inclusive, decay_row, 0.0), axis=2, keepdims=True)
        spread = cum - cum_row
        fade = jnp.where(inclusive, jnp.exp(jnp.where(inclusive, spread, 0.0)), 0.0)
        key_dot = bdot_nt(k, k) * (k_norm * k_norm_row)
        query_dot = bdot_nt(q, k) * (q_norm * k_norm_row)
        negated = jnp.where(lower, -(strength * key_dot * fade), 0.0)
        base = jnp.where(same(8), negated, 0.0)
        inverse = identity + base
        powered = bdot3(base, base)
        inverse = inverse + bdot3(inverse, powered)
        powered = bdot3(powered, powered)
        inverse = inverse + bdot3(inverse, powered)
        for size in (8, 16, 32):
            cross = jnp.where(same(2 * size) & ~same(size), negated, 0.0).astype(BF16)
            half = inverse.astype(BF16)
            inverse = inverse + bdot_nn(bdot_nn(half, cross).astype(BF16), half)
        inverse_half = inverse.astype(BF16)
        decay_gain = jnp.exp(cum)
        last = cum[:, BLOCK - 1 : BLOCK, :]
        tail = jnp.exp(last - cum)
        unit_k = k_norm * kf
        w = bdot_nn(inverse_half, ((strength * decay_gain) * unit_k).astype(BF16)).astype(BF16)
        v_t = bdot_nt(wide_eye, v) * strength_row
        u_t = bdot_nt(v_t.astype(BF16), inverse_half)
        scores = (query_dot * fade).astype(BF16)
        q_part = decay_gain * (q_norm * qf) - bdot_nn(scores, w)
        local = bdot_nt(scores, u_t.astype(BF16))
        w_ref[pl.ds(start, GROUP)] = w
        u_ref[pl.ds(start, GROUP)] = u_t
        k_ref[pl.ds(start, GROUP)] = (tail * unit_k).astype(BF16)
        gain_ref[pl.ds(start, GROUP)] = jnp.broadcast_to(jnp.exp(last), (GROUP, 8, 128))
        query_part_ref[pl.ds(start, GROUP)] = q_part.astype(BF16)
        local_ref[pl.ds(start, GROUP)] = local
        return unused

    lax.fori_loop(0, BLOCKS // GROUP, parts, 0)

    map_row = lax.broadcasted_iota(jnp.int32, (MAP_ROWS, DH), 0)
    map_col = lax.broadcasted_iota(jnp.int32, (MAP_ROWS, DH), 1)
    diagonal = map_row == map_col
    start_map = jnp.where(diagonal, 1.0, 0.0).astype(F32)

    def advance(step, carried):
        maps, gains = carried
        new_maps, new_gains = [], []
        for chunk in range(CHUNKS):
            index = chunk * STEPS + step
            state = maps[chunk]
            half = state.astype(BF16)
            out = dot_nt(query_part_ref[index], half)
            seen = dot_nt(half, w_ref[index])
            fresh = jnp.concatenate([-seen[0:DH], u_ref[index] - seen[DH:MAP_ROWS]], axis=0)
            gain = gain_ref[index][0:1, :]
            query_part_ref[index] = out[:, 0:DH].astype(BF16)
            local_ref[index] = local_ref[index] + out[:, DH:MAP_ROWS]
            new_maps.append(gain * state + dot_nn(fresh.astype(BF16), k_ref[index]))
            new_gains.append(gain * gains[chunk])
        return tuple(new_maps), tuple(new_gains)

    maps, gains = lax.fori_loop(
        0,
        STEPS,
        advance,
        (
            tuple(start_map for _ in range(CHUNKS)),
            tuple(jnp.ones((1, DH), F32) for _ in range(CHUNKS)),
        ),
    )
    whole = None
    for chunk in range(CHUNKS):
        gain = gains[chunk]
        changed = maps[chunk] - jnp.where(diagonal, gain, 0.0)
        sub_map_ref[chunk] = changed
        sub_gain_ref[chunk] = jnp.broadcast_to(gain, (8, DH))
        if whole is None:
            whole, total = maps[chunk], gain
        else:
            added = jnp.where(map_row < DH, 0.0, changed)
            whole = gain * whole + dot_nn(whole.astype(BF16), changed[0:DH].astype(BF16)) + added
            total = gain * total
    send_ref[0:MAP_ROWS, :] = (whole - jnp.where(diagonal, total, 0.0)).astype(BF16)
    high, low = spread_gain(total)
    send_ref[MAP_ROWS : MAP_ROWS + 16, :] = high
    send_ref[MAP_ROWS + 16 : MAP_ROWS + 32, :] = low


def compose_kernel(half_ref, own_ref, other_ref, out_ref):
    map_row = lax.broadcasted_iota(jnp.int32, (MAP_ROWS, DH), 0)
    map_col = lax.broadcasted_iota(jnp.int32, (MAP_ROWS, DH), 1)
    diagonal = map_row == map_col

    def emit(first_ref, second_ref, start):
        gain_first = read_gain(first_ref[MAP_ROWS : MAP_ROWS + 16], first_ref[MAP_ROWS + 16 : MAP_ROWS + 32])
        gain = read_gain(second_ref[MAP_ROWS : MAP_ROWS + 16], second_ref[MAP_ROWS + 16 : MAP_ROWS + 32])
        total = gain * gain_first
        first = first_ref[0:MAP_ROWS, :].astype(F32) + jnp.where(diagonal, gain_first, 0.0)
        second = second_ref[0:MAP_ROWS, :].astype(F32)
        whole = gain * first + dot_nn(first.astype(BF16), second_ref[0:DH, :])
        whole = whole + jnp.where(map_row < DH, 0.0, second) - jnp.where(diagonal, total, 0.0)
        out_ref[0:DH, :] = whole[0:DH].astype(BF16)
        out_ref[DH : DH + WIDTH, :] = whole[DH + start : DH + start + WIDTH].astype(BF16)
        high, low = spread_gain(total)
        out_ref[DH + WIDTH : DH + WIDTH + 16, :] = high
        out_ref[DH + WIDTH + 16 : DH + WIDTH + 32, :] = low

    @pl.when(half_ref[0] == 0)
    def _():
        emit(own_ref, other_ref, 0)

    @pl.when(half_ref[0] != 0)
    def _():
        emit(other_ref, own_ref, WIDTH)


def fold_kernel(position_ref, maps_ref, out_ref):
    def fold(index, state):
        gain = read_gain(
            maps_ref[index, DH + WIDTH : DH + WIDTH + 16, :],
            maps_ref[index, DH + WIDTH + 16 : DH + WIDTH + 32, :],
        )
        return (
            gain * state
            + dot_nn(state.astype(BF16), maps_ref[index, 0:DH, :])
            + maps_ref[index, DH : DH + WIDTH, :].astype(F32)
        )

    out_ref[...] = lax.fori_loop(0, position_ref[0], fold, jnp.zeros((WIDTH, DH), F32))


def head_kernel(
    half_ref,
    own_ref,
    other_ref,
    other_map_ref,
    query_part_ref,
    local_ref,
    sub_map_ref,
    sub_gain_ref,
    out_ref,
    state_ref,
):
    @pl.when(half_ref[0] == 0)
    def _():
        state_ref[0:WIDTH, :] = own_ref[...]
        state_ref[WIDTH:DH, :] = other_ref[...]

    @pl.when(half_ref[0] != 0)
    def _():
        state = jnp.concatenate([other_ref[...], own_ref[...]], axis=0)
        gain = read_gain(
            other_map_ref[MAP_ROWS : MAP_ROWS + 16, :], other_map_ref[MAP_ROWS + 16 : MAP_ROWS + 32, :]
        )
        state_ref[...] = (
            gain * state
            + dot_nn(state.astype(BF16), other_map_ref[0:DH, :])
            + other_map_ref[DH:MAP_ROWS, :].astype(F32)
        )

    state = state_ref[...]
    for chunk in range(CHUNKS):
        half = state.astype(BF16)
        for step in range(STEPS):
            index = chunk * STEPS + step
            out_ref[index] = (dot_nt(query_part_ref[index], half) + local_ref[index]).astype(BF16)
        if chunk + 1 < CHUNKS:
            changed = sub_map_ref[chunk]
            state = (
                sub_gain_ref[chunk][0:1] * state
                + dot_nn(half, changed[0:DH].astype(BF16))
                + changed[DH:MAP_ROWS]
            )


def mixed_kernel(
    tok_ref, heads_ref, residual_ref, out_gain_ref, ffn_gain_ref, mixed_ref, send_ref, rows_ref
):
    gain = out_gain_ref[...]
    total = jnp.zeros((TOK, 1), F32)
    for head in range(VALUE_HEADS):
        wide = heads_ref[head].astype(F32)
        scale = lax.rsqrt(jnp.mean(wide * wide, axis=1, keepdims=True) + 1e-06)
        part = slice(head * DH, head * DH + DH)
        mixed = (residual_ref[:, part].astype(F32) + wide * scale * gain).astype(BF16)
        mixed_ref[:, part] = mixed
        mixed_wide = mixed.astype(F32)
        total = total + jnp.sum(mixed_wide * mixed_wide, axis=1, keepdims=True)
    scale = lax.rsqrt(total * (1.0 / D) + 1e-06)
    swap = swap_matrix()
    for group in range(TOK // 16):
        tokens = slice(group * 16, group * 16 + 16)
        pieces = []
        for c in range(COLS):
            part = slice(c * 128, c * 128 + 128)
            value = mixed_ref[tokens, part].astype(F32) * scale[tokens] * ffn_gain_ref[:, part]
            pieces.append(value.astype(BF16))
        swapped = dot_nn(swap, jnp.concatenate(pieces, axis=0)).astype(BF16)
        rows_ref[tokens] = swapped.reshape(16, 16, 128)

    def place(expert, unused):
        send_ref[2 * expert] = rows_ref[tok_ref[0, expert]]
        send_ref[2 * expert + 1] = rows_ref[tok_ref[1, expert]]
        return unused

    lax.fori_loop(0, EXPERTS, place, 0, unroll=16)


FFN_ROWS = 256


def expert_kernel(rows_ref, gate_ref, up_ref, down_ref, out_ref, wide_ref):
    swap = swap_matrix()
    for pair in range(FFN_ROWS // 32):
        start = pair * 512
        rows = [rows_ref[start : start + 256, :], rows_ref[start + 256 : start + 512, :]]
        tile = dot_nn(swap, jnp.concatenate(rows, axis=1)).astype(BF16)
        for c in range(COLS):
            part = slice(c * 128, c * 128 + 128)
            wide_ref[pair * 32 : pair * 32 + 16, part] = tile[c * 16 : c * 16 + 16, 0:128]
            wide_ref[pair * 32 + 16 : pair * 32 + 32, part] = tile[c * 16 : c * 16 + 16, 128:256]
    wide = wide_ref[...]
    gate = dot_nn(wide, gate_ref[...])
    up = dot_nn(wide, up_ref[...])
    hidden = (gate / (1.0 + jnp.exp(-gate)) * up).astype(BF16)
    wide_ref[...] = dot_nn(hidden, down_ref[...]).astype(BF16)
    for pair in range(FFN_ROWS // 32):
        sides = []
        for start in (pair * 32, pair * 32 + 16):
            pieces = [wide_ref[start : start + 16, c * 128 : c * 128 + 128] for c in range(COLS)]
            sides.append(jnp.concatenate(pieces, axis=0))
        tile = dot_nn(swap, jnp.concatenate(sides, axis=1)).astype(BF16)
        out_ref[pair * 512 : pair * 512 + 256, :] = tile[:, 0:128]
        out_ref[pair * 512 + 256 : pair * 512 + 512, :] = tile[:, 128:256]


def combine_kernel(slot_ref, weight_ref, rows_ref, out_ref, sum_ref):
    def token(index, unused):
        total = jnp.zeros((16, 128), F32)
        for k in range(TOPK):
            total = total + weight_ref[index, k] * rows_ref[slot_ref[index, k]].astype(F32)
        sum_ref[index] = total.astype(BF16)
        return unused

    lax.fori_loop(0, TOK, token, 0, unroll=2)
    swap = swap_matrix()
    for group in range(TOK // 16):
        tokens = slice(group * 16, group * 16 + 16)
        tile = dot_nn(swap, sum_ref[tokens].reshape(256, 128)).astype(BF16)
        for c in range(COLS):
            out_ref[tokens, c * 128 : c * 128 + 128] = tile[c * 16 : c * 16 + 16]


def shape(dims, dtype):
    return jax.ShapeDtypeStruct(dims, dtype)


SMEM = pl.BlockSpec(memory_space=pltpu.SMEM)
WHOLE = pl.BlockSpec(memory_space=pltpu.VMEM)


def pack(query, key, value, decay, strength):
    return pl.pallas_call(
        pack_kernel,
        out_shape=shape((VALUE_HEADS, PACK_ROWS, 128), BF16),
        in_specs=[WHOLE] * 5,
        out_specs=WHOLE,
        compiler_params=params(),
        name="pack",
    )(query, key, value, decay, strength)


def route(ids, weights):
    return pl.pallas_call(
        route_kernel,
        out_shape=(
            shape((2, EXPERTS), jnp.int32),
            shape((TOK, 128), jnp.int32),
            shape((TOK, 128), F32),
        ),
        in_specs=[WHOLE, WHOLE],
        out_specs=(WHOLE, WHOLE, WHOLE),
        compiler_params=params(),
        name="route",
    )(ids, weights)


def mixer(received):
    return pl.pallas_call(
        mixer_kernel,
        out_shape=(
            shape((BLOCKS, BLOCK, DH), BF16),
            shape((BLOCKS, BLOCK, DH), F32),
            shape((CHUNKS, MAP_ROWS, DH), F32),
            shape((CHUNKS, 8, DH), F32),
            shape((HALF_ROWS, DH), BF16),
        ),
        in_specs=[WHOLE],
        out_specs=(WHOLE,) * 5,
        scratch_shapes=[
            pltpu.VMEM((BLOCKS, BLOCK, DH), BF16),
            pltpu.VMEM((BLOCKS, DH, BLOCK), F32),
            pltpu.VMEM((BLOCKS, BLOCK, DH), BF16),
            pltpu.VMEM((BLOCKS, 8, DH), F32),
        ],
        compiler_params=params(),
        name="mixer",
    )(received)


def compose(half, own, other):
    return pl.pallas_call(
        compose_kernel,
        out_shape=shape((SEG_ROWS, DH), BF16),
        in_specs=[SMEM, WHOLE, WHOLE],
        out_specs=WHOLE,
        compiler_params=params(),
        name="compose",
    )(half, own, other)


def fold(position, maps):
    return pl.pallas_call(
        fold_kernel,
        out_shape=shape((WIDTH, DH), F32),
        in_specs=[SMEM, WHOLE],
        out_specs=WHOLE,
        compiler_params=params(),
        name="fold",
    )(position, maps)


def head_rows(half, own, other, other_map, query_part, local, sub_map, sub_gain):
    return pl.pallas_call(
        head_kernel,
        out_shape=shape((BLOCKS, BLOCK, DH), BF16),
        in_specs=[SMEM] + [WHOLE] * 7,
        out_specs=WHOLE,
        scratch_shapes=[pltpu.VMEM((DH, DH), F32)],
        compiler_params=params(),
        name="heads",
    )(half, own, other, other_map, query_part, local, sub_map, sub_gain)


def mix(tok, heads, residual, out_gain, ffn_gain):
    return pl.pallas_call(
        mixed_kernel,
        out_shape=(shape((TOK, D), BF16), shape((SLOTS, 16, 128), BF16)),
        in_specs=[SMEM] + [WHOLE] * 4,
        out_specs=(WHOLE, WHOLE),
        scratch_shapes=[pltpu.VMEM((TOK, 16, 128), BF16)],
        compiler_params=params(),
        name="mix",
    )(tok, heads, residual, out_gain, ffn_gain)


def experts(rows, gate, up, down):
    hidden = gate.shape[1]
    block = pl.BlockSpec((FFN_ROWS * 16, 128), lambda i: (i, 0))
    return pl.pallas_call(
        expert_kernel,
        grid=(SLOTS // FFN_ROWS,),
        out_shape=shape((SLOTS * 16, 128), BF16),
        in_specs=[
            block,
            pl.BlockSpec((D, hidden), lambda i: (0, 0)),
            pl.BlockSpec((D, hidden), lambda i: (0, 0)),
            pl.BlockSpec((hidden, D), lambda i: (0, 0)),
        ],
        out_specs=block,
        scratch_shapes=[pltpu.VMEM((FFN_ROWS, D), BF16)],
        compiler_params=params(),
        name="experts",
    )(rows, gate, up, down)


def combine(slots, weights, rows):
    return pl.pallas_call(
        combine_kernel,
        out_shape=shape((TOK, D), BF16),
        in_specs=[SMEM, SMEM, WHOLE],
        out_specs=WHOLE,
        scratch_shapes=[pltpu.VMEM((TOK, 16, 128), BF16)],
        compiler_params=params(),
        name="combine",
    )(slots, weights, rows)


def swap_all(x, axes):
    return lax.all_to_all(x, axes, split_axis=0, concat_axis=0, tiled=True)


def trade(x):
    return lax.ppermute(x, "half", [(0, 1), (1, 0)])


HEAD_AXES = ("pair", "y")
SEQ_AXES = ("half", "pair", "y")
EXP_AXES = ("z", "core")


def body(
    mixer_query,
    mixer_key,
    mixer_value,
    log_decay,
    strength,
    residual,
    out_gain,
    ffn_gain,
    expert_ids,
    expert_weights,
    gate_proj,
    up_proj,
    down_proj,
):
    sent = pack(mixer_query[0], mixer_key[0], mixer_value[0], log_decay[0].T, strength[0].T)
    received = swap_all(sent, HEAD_AXES)
    tok, slots, weights = route(expert_ids[0], expert_weights[0])
    half = lax.axis_index("half").astype(jnp.int32).reshape(1)
    position = lax.axis_index(EXP_AXES).astype(jnp.int32).reshape(1)
    query_part, local, sub_map, sub_gain, own_map = mixer(received)
    other_map = trade(own_map)
    maps = lax.all_gather(compose(half, own_map, other_map), EXP_AXES, axis=0)
    own_state = fold(position, maps)
    other_state = trade(own_state)
    outs = head_rows(half, own_state, other_state, other_map, query_part, local, sub_map, sub_gain)
    heads = swap_all(outs, HEAD_AXES)
    mixed, outgoing = mix(
        tok, heads, residual[0], out_gain.reshape(1, DH), ffn_gain.reshape(1, D)
    )
    arrived = swap_all(outgoing, SEQ_AXES + EXP_AXES)
    result = experts(arrived.reshape(SLOTS * 16, 128), gate_proj[0], up_proj[0], down_proj[0])
    returned = swap_all(result.reshape(SLOTS, 16, 128), SEQ_AXES + EXP_AXES)
    ffn_out = combine(slots, weights, returned)
    return (mixed[None], ffn_out[None])


def solution(mesh):
    fine = Mesh(mesh.devices.reshape(2, 2, 8, 8, 2), SEQ_AXES + EXP_AXES)
    rows = P(EXP_AXES, SEQ_AXES, None)
    owned = P(SEQ_AXES + EXP_AXES, None, None)
    return jax.shard_map(
        body,
        mesh=fine,
        in_specs=(rows,) * 6 + (P(), P(), rows, rows) + (owned,) * 3,
        out_specs=(rows, rows),
        check_vma=False,
    )
```

```python
import jax
import jax.numpy as jnp
from jax import lax
from jax.experimental import pallas as pl
from jax.experimental.pallas import tpu as pltpu
from jax.sharding import Mesh
from jax.sharding import PartitionSpec as P

D = 2048
DH = 128
HK = 8
VALUE_HEADS = 16
TOPK = 10
BLOCK = 64
TOK = 64
EXPERTS = 512
WIDTH = 64
BLOCKS = 16
GROUP = 8
CHUNKS = 4
STEPS = 4
PACK_ROWS = 3 * TOK + 16
MAP_ROWS = 2 * DH
HALF_ROWS = MAP_ROWS + 32
SEG_ROWS = DH + WIDTH + 32
SLOTS = 2 * EXPERTS
COLS = D // 128
F32 = jnp.float32
BF16 = jnp.bfloat16
VMEM_LIMIT = 16 * 1024 * 1024


def params():
    return pltpu.CompilerParams(vmem_limit_bytes=VMEM_LIMIT)


def full(*arrays):
    return [pl.BlockSpec(memory_space=pltpu.VMEM) for _ in arrays]


def dot_nn(a, b):
    return lax.dot_general(a, b, (((1,), (0,)), ((), ())), preferred_element_type=F32)


def dot_nt(a, b):
    return lax.dot_general(a, b, (((1,), (1,)), ((), ())), preferred_element_type=F32)


def bdot_nn(a, b):
    return lax.dot_general(a, b, (((2,), (1,)), ((0,), (0,))), preferred_element_type=F32)


def bdot_nt(a, b):
    return lax.dot_general(a, b, (((2,), (2,)), ((0,), (0,))), preferred_element_type=F32)


def split(x):
    high = x.astype(BF16)
    return high, (x - high.astype(F32)).astype(BF16)


def bdot3(a, b):
    ah, al = split(a)
    bh, bl = split(b)
    return bdot_nn(ah, bh) + (bdot_nn(ah, bl) + bdot_nn(al, bh))


def swap_matrix():
    out_index = lax.broadcasted_iota(jnp.int32, (256, 256), 0)
    in_index = lax.broadcasted_iota(jnp.int32, (256, 256), 1)
    return (in_index == (out_index % 16) * 16 + out_index // 16).astype(BF16)


def pack_kernel(
    half_ref,
    query_ref,
    key_ref,
    value_ref,
    decay_ref,
    strength_ref,
    out_ref,
    decay_rows,
    strength_rows,
    sems,
):
    gate_copies = [
        pltpu.make_async_copy(decay_ref, decay_rows, sems.at[3, 0]),
        pltpu.make_async_copy(strength_ref, strength_rows, sems.at[3, 1]),
    ]
    copies = []
    for head in range(VALUE_HEADS):
        place = lax.rem(head + half_ref[0] * 8, VALUE_HEADS)
        for part, (ref, column) in enumerate(
            ((query_ref, head // 2), (key_ref, head // 2), (value_ref, head))
        ):
            copies.append(
                pltpu.make_async_copy(
                    ref.at[:, column * DH : column * DH + DH],
                    out_ref.at[place, part * TOK : part * TOK + TOK, :],
                    sems.at[part, head],
                )
            )
    for copy in gate_copies + copies:
        copy.start()
    for copy in gate_copies:
        copy.wait()
    gates = jnp.concatenate([decay_rows[...].astype(F32), strength_rows[...].astype(F32)], axis=1)
    for head in range(VALUE_HEADS):
        place = lax.rem(head + half_ref[0] * 8, VALUE_HEADS)
        out_ref[place, 192:208, :] = jnp.broadcast_to(gates[head : head + 1], (16, 128)).astype(BF16)
    for copy in copies:
        copy.wait()


def route_kernel(ids_ref, weight_in_ref, tok_ref, slot_ref, weight_ref):
    expert = lax.broadcasted_iota(jnp.int32, (TOK, EXPERTS), 1)
    named = jnp.zeros((TOK, EXPERTS), F32)
    for k in range(TOPK):
        named = jnp.where(ids_ref[:, k : k + 1] == expert, 1.0, named)
    row = lax.broadcasted_iota(jnp.int32, (TOK, TOK), 0)
    col = lax.broadcasted_iota(jnp.int32, (TOK, TOK), 1)
    rank = dot_nn((row > col).astype(BF16), named.astype(BF16))
    token = lax.broadcasted_iota(jnp.int32, (TOK, EXPERTS), 0).astype(F32)
    first = jnp.sum(jnp.where(rank == 0.0, token * named, 0.0), axis=0, keepdims=True)
    second = jnp.sum(jnp.where(rank == 1.0, token * named, 0.0), axis=0, keepdims=True)
    tok_ref[...] = jnp.concatenate([first, second], axis=0).astype(jnp.int32)
    lane = lax.broadcasted_iota(jnp.int32, (TOK, 128), 1)
    slots = jnp.zeros((TOK, 128), jnp.int32)
    weights = jnp.zeros((TOK, 128), F32)
    for k in range(TOPK):
        ids = ids_ref[:, k : k + 1]
        mine = jnp.sum(jnp.where(ids == expert, rank, 0.0), axis=1, keepdims=True)
        slots = jnp.where(lane == k, 2 * ids + mine.astype(jnp.int32), slots)
        weights = jnp.where(lane == k, weight_in_ref[:, k : k + 1], weights)
    slot_ref[...] = slots
    weight_ref[...] = weights


def spread_gain(gain):
    high, low = split(gain)
    rows = (16, DH)
    return (
        jnp.broadcast_to(high.astype(F32), rows).astype(BF16),
        jnp.broadcast_to(low.astype(F32), rows).astype(BF16),
    )


def read_gain(high, low):
    return (high.astype(F32) + low.astype(F32))[0:1]


def mixer_kernel(
    recv_ref,
    next_gate_ref,
    next_up_ref,
    next_down_ref,
    query_part_ref,
    local_ref,
    sub_map_ref,
    sub_gain_ref,
    send_ref,
    w_ref,
    u_ref,
    k_ref,
    gain_ref,
):
    row = lax.broadcasted_iota(jnp.int32, (BLOCK, BLOCK), 0)
    col = lax.broadcasted_iota(jnp.int32, (BLOCK, BLOCK), 1)
    eye = (row == col)[None]
    inclusive = (row >= col)[None]
    upper = (row <= col)[None]
    lower = (row > col)[None]

    def same(size):
        return ((row // size) == (col // size))[None]

    identity = jnp.broadcast_to(eye.astype(F32), (GROUP, BLOCK, BLOCK))
    wide_row = lax.broadcasted_iota(jnp.int32, (DH, DH), 0)
    wide_col = lax.broadcasted_iota(jnp.int32, (DH, DH), 1)
    wide_eye = jnp.broadcast_to((wide_row == wide_col).astype(F32)[None], (GROUP, DH, DH)).astype(BF16)

    def parts(step, unused):
        start = step * GROUP
        block = recv_ref[pl.ds(start, GROUP)]
        q = block[:, 0:64]
        k = block[:, 64:128]
        v = block[:, 128:192]
        gates = block[:, 192:208].astype(F32)
        decay_row = gates[:, 0:1, 0:64]
        strength_row = gates[:, 0:1, 64:128]
        qf = q.astype(F32)
        kf = k.astype(F32)
        q_norm = lax.rsqrt(jnp.sum(qf * qf, axis=2, keepdims=True) + 1e-06)
        k_norm = lax.rsqrt(jnp.sum(kf * kf, axis=2, keepdims=True) + 1e-06)
        k_norm_row = jnp.sum(jnp.where(eye, k_norm, 0.0), axis=1, keepdims=True)
        decay = jnp.sum(jnp.where(eye, decay_row, 0.0), axis=2, keepdims=True)
        strength = jnp.sum(jnp.where(eye, strength_row, 0.0), axis=2, keepdims=True)
        cum_row = jnp.sum(jnp.where(upper, decay, 0.0), axis=1, keepdims=True)
        cum = jnp.sum(jnp.where(inclusive, decay_row, 0.0), axis=2, keepdims=True)
        spread = cum - cum_row
        fade = jnp.where(inclusive, jnp.exp(jnp.where(inclusive, spread, 0.0)), 0.0)
        key_dot = bdot_nt(k, k) * (k_norm * k_norm_row)
        query_dot = bdot_nt(q, k) * (q_norm * k_norm_row)
        negated = jnp.where(lower, -(strength * key_dot * fade), 0.0)
        base = jnp.where(same(8), negated, 0.0)
        inverse = identity + base
        powered = bdot3(base, base)
        inverse = inverse + bdot3(inverse, powered)
        powered = bdot3(powered, powered)
        inverse = inverse + bdot3(inverse, powered)
        for size in (8, 16, 32):
            cross = jnp.where(same(2 * size) & ~same(size), negated, 0.0).astype(BF16)
            half = inverse.astype(BF16)
            inverse = inverse + bdot_nn(bdot_nn(half, cross).astype(BF16), half)
        inverse_half = inverse.astype(BF16)
        decay_gain = jnp.exp(cum)
        last = cum[:, BLOCK - 1 : BLOCK, :]
        tail = jnp.exp(last - cum)
        unit_k = k_norm * kf
        w = bdot_nn(inverse_half, ((strength * decay_gain) * unit_k).astype(BF16)).astype(BF16)
        v_t = bdot_nt(wide_eye, v) * strength_row
        u_t = bdot_nt(v_t.astype(BF16), inverse_half)
        scores = (query_dot * fade).astype(BF16)
        q_part = decay_gain * (q_norm * qf) - bdot_nn(scores, w)
        local = bdot_nt(scores, u_t.astype(BF16))
        w_ref[pl.ds(start, GROUP)] = w
        u_ref[pl.ds(start, GROUP)] = u_t
        k_ref[pl.ds(start, GROUP)] = (tail * unit_k).astype(BF16)
        gain_ref[pl.ds(start, GROUP)] = jnp.broadcast_to(jnp.exp(last), (GROUP, 8, 128))
        query_part_ref[pl.ds(start, GROUP)] = q_part.astype(BF16)
        local_ref[pl.ds(start, GROUP)] = local
        return unused

    lax.fori_loop(0, BLOCKS // GROUP, parts, 0)

    map_row = lax.broadcasted_iota(jnp.int32, (MAP_ROWS, DH), 0)
    map_col = lax.broadcasted_iota(jnp.int32, (MAP_ROWS, DH), 1)
    diagonal = map_row == map_col
    start_map = jnp.where(diagonal, 1.0, 0.0).astype(F32)

    def advance(step, carried):
        maps, gains = carried
        new_maps, new_gains = [], []
        for chunk in range(CHUNKS):
            index = chunk * STEPS + step
            state = maps[chunk]
            half = state.astype(BF16)
            out = dot_nt(query_part_ref[index], half)
            seen = dot_nt(half, w_ref[index])
            fresh = jnp.concatenate([-seen[0:DH], u_ref[index] - seen[DH:MAP_ROWS]], axis=0)
            gain = gain_ref[index][0:1, :]
            query_part_ref[index] = out[:, 0:DH].astype(BF16)
            local_ref[index] = local_ref[index] + out[:, DH:MAP_ROWS]
            new_maps.append(gain * state + dot_nn(fresh.astype(BF16), k_ref[index]))
            new_gains.append(gain * gains[chunk])
        return tuple(new_maps), tuple(new_gains)

    maps, gains = lax.fori_loop(
        0,
        STEPS,
        advance,
        (
            tuple(start_map for _ in range(CHUNKS)),
            tuple(jnp.ones((1, DH), F32) for _ in range(CHUNKS)),
        ),
    )
    whole = None
    for chunk in range(CHUNKS):
        gain = gains[chunk]
        changed = maps[chunk] - jnp.where(diagonal, gain, 0.0)
        sub_map_ref[chunk] = changed
        sub_gain_ref[chunk] = jnp.broadcast_to(gain, (8, DH))
        if whole is None:
            whole, total = maps[chunk], gain
        else:
            added = jnp.where(map_row < DH, 0.0, changed)
            whole = gain * whole + dot_nn(whole.astype(BF16), changed[0:DH].astype(BF16)) + added
            total = gain * total
    send_ref[0:MAP_ROWS, :] = (whole - jnp.where(diagonal, total, 0.0)).astype(BF16)
    high, low = spread_gain(total)
    send_ref[MAP_ROWS : MAP_ROWS + 16, :] = high
    send_ref[MAP_ROWS + 16 : MAP_ROWS + 32, :] = low


def compose_kernel(half_ref, own_ref, other_ref, out_ref):
    map_row = lax.broadcasted_iota(jnp.int32, (MAP_ROWS, DH), 0)
    map_col = lax.broadcasted_iota(jnp.int32, (MAP_ROWS, DH), 1)
    diagonal = map_row == map_col

    def emit(first_ref, second_ref, start):
        gain_first = read_gain(first_ref[MAP_ROWS : MAP_ROWS + 16], first_ref[MAP_ROWS + 16 : MAP_ROWS + 32])
        gain = read_gain(second_ref[MAP_ROWS : MAP_ROWS + 16], second_ref[MAP_ROWS + 16 : MAP_ROWS + 32])
        total = gain * gain_first
        first = first_ref[0:MAP_ROWS, :].astype(F32) + jnp.where(diagonal, gain_first, 0.0)
        second = second_ref[0:MAP_ROWS, :].astype(F32)
        whole = gain * first + dot_nn(first.astype(BF16), second_ref[0:DH, :])
        whole = whole + jnp.where(map_row < DH, 0.0, second) - jnp.where(diagonal, total, 0.0)
        out_ref[0:DH, :] = whole[0:DH].astype(BF16)
        out_ref[DH : DH + WIDTH, :] = whole[DH + start : DH + start + WIDTH].astype(BF16)
        high, low = spread_gain(total)
        out_ref[DH + WIDTH : DH + WIDTH + 16, :] = high
        out_ref[DH + WIDTH + 16 : DH + WIDTH + 32, :] = low

    @pl.when(half_ref[0] == 0)
    def _():
        emit(own_ref, other_ref, 0)

    @pl.when(half_ref[0] != 0)
    def _():
        emit(other_ref, own_ref, WIDTH)


def fold_kernel(position_ref, maps_ref, out_ref):
    def fold(index, state):
        gain = read_gain(
            maps_ref[index, DH + WIDTH : DH + WIDTH + 16, :],
            maps_ref[index, DH + WIDTH + 16 : DH + WIDTH + 32, :],
        )
        return (
            gain * state
            + dot_nn(state.astype(BF16), maps_ref[index, 0:DH, :])
            + maps_ref[index, DH : DH + WIDTH, :].astype(F32)
        )

    out_ref[...] = lax.fori_loop(0, position_ref[0], fold, jnp.zeros((WIDTH, DH), F32))


def head_kernel(
    half_ref,
    own_ref,
    other_ref,
    other_map_ref,
    query_part_ref,
    local_ref,
    sub_map_ref,
    sub_gain_ref,
    out_ref,
    state_ref,
):
    @pl.when(half_ref[0] == 0)
    def _():
        state_ref[0:WIDTH, :] = own_ref[...]
        state_ref[WIDTH:DH, :] = other_ref[...]

    @pl.when(half_ref[0] != 0)
    def _():
        state = jnp.concatenate([other_ref[...], own_ref[...]], axis=0)
        gain = read_gain(
            other_map_ref[MAP_ROWS : MAP_ROWS + 16, :], other_map_ref[MAP_ROWS + 16 : MAP_ROWS + 32, :]
        )
        state_ref[...] = (
            gain * state
            + dot_nn(state.astype(BF16), other_map_ref[0:DH, :])
            + other_map_ref[DH:MAP_ROWS, :].astype(F32)
        )

    state = state_ref[...]
    for chunk in range(CHUNKS):
        half = state.astype(BF16)
        for step in range(STEPS):
            index = chunk * STEPS + step
            out_ref[index] = (dot_nt(query_part_ref[index], half) + local_ref[index]).astype(BF16)
        if chunk + 1 < CHUNKS:
            changed = sub_map_ref[chunk]
            state = (
                sub_gain_ref[chunk][0:1] * state
                + dot_nn(half, changed[0:DH].astype(BF16))
                + changed[DH:MAP_ROWS]
            )


def mixed_kernel(
    half_ref,
    tok_ref,
    heads_ref,
    residual_ref,
    out_gain_ref,
    ffn_gain_ref,
    mixed_ref,
    send_ref,
    rows_ref,
):
    gain = out_gain_ref[...]
    total = jnp.zeros((TOK, 1), F32)
    for head in range(VALUE_HEADS):
        wide = heads_ref[lax.rem(head + half_ref[0] * 8, VALUE_HEADS)].astype(F32)
        scale = lax.rsqrt(jnp.mean(wide * wide, axis=1, keepdims=True) + 1e-06)
        part = slice(head * DH, head * DH + DH)
        mixed = (residual_ref[:, part].astype(F32) + wide * scale * gain).astype(BF16)
        mixed_ref[:, part] = mixed
        mixed_wide = mixed.astype(F32)
        total = total + jnp.sum(mixed_wide * mixed_wide, axis=1, keepdims=True)
    scale = lax.rsqrt(total * (1.0 / D) + 1e-06)
    swap = swap_matrix()
    for group in range(TOK // 16):
        tokens = slice(group * 16, group * 16 + 16)
        pieces = []
        for c in range(COLS):
            part = slice(c * 128, c * 128 + 128)
            value = mixed_ref[tokens, part].astype(F32) * scale[tokens] * ffn_gain_ref[:, part]
            pieces.append(value.astype(BF16))
        swapped = dot_nn(swap, jnp.concatenate(pieces, axis=0)).astype(BF16)
        rows_ref[tokens] = swapped.reshape(16, 16, 128)

    def place(expert, unused):
        send_ref[2 * expert] = rows_ref[tok_ref[0, expert]]
        send_ref[2 * expert + 1] = rows_ref[tok_ref[1, expert]]
        return unused

    lax.fori_loop(0, EXPERTS, place, 0, unroll=16)


FFN_ROWS = 256
CHIPS = EXPERTS // 2


def expert_kernel(core_ref, rows_ref, *refs):
    weight_refs, (out_ref, wide_ref) = refs[:6], refs[6:]
    swap = swap_matrix()

    def spread(start):
        return rows_ref[start : start + 8].reshape(256, 128)

    for pair in range(FFN_ROWS // 32):
        rows = [spread(pair * 16), spread(pair * 16 + 8)]
        tile = dot_nn(swap, jnp.concatenate(rows, axis=1)).astype(BF16)
        for c in range(COLS):
            part = slice(c * 128, c * 128 + 128)
            wide_ref[pair * 32 : pair * 32 + 16, part] = tile[c * 16 : c * 16 + 16, 0:128]
            wide_ref[pair * 32 + 16 : pair * 32 + 32, part] = tile[c * 16 : c * 16 + 16, 128:256]

    def expert(gate_ref, up_ref, down_ref):
        wide = wide_ref[...]
        gate = dot_nn(wide, gate_ref[...])
        up = dot_nn(wide, up_ref[...])
        hidden = (gate / (1.0 + jnp.exp(-gate)) * up).astype(BF16)
        wide_ref[...] = dot_nn(hidden, down_ref[...]).astype(BF16)

    for which in range(2):

        @pl.when(pl.program_id(0) == which)
        def _(which=which):
            expert(*weight_refs[which * 3 : which * 3 + 3])

    for pair in range(FFN_ROWS // 32):
        sides = []
        for start in (pair * 32, pair * 32 + 16):
            pieces = [wide_ref[start : start + 16, c * 128 : c * 128 + 128] for c in range(COLS)]
            sides.append(jnp.concatenate(pieces, axis=0))
        tile = dot_nn(swap, jnp.concatenate(sides, axis=1)).astype(BF16)
        out_ref[pair * 16 : pair * 16 + 8] = tile[:, 0:128].reshape(8, 1, 32, 128)
        out_ref[pair * 16 + 8 : pair * 16 + 16] = tile[:, 128:256].reshape(8, 1, 32, 128)


def combine_kernel(slot_ref, weight_ref, rows_ref, out_ref, sum_ref):
    def token(index, unused):
        total = jnp.zeros((16, 128), F32)
        for k in range(TOPK):
            total = total + weight_ref[index, k] * rows_ref[slot_ref[index, k]].astype(F32)
        sum_ref[index] = total.astype(BF16)
        return unused

    lax.fori_loop(0, TOK, token, 0, unroll=2)
    swap = swap_matrix()
    for group in range(TOK // 16):
        tokens = slice(group * 16, group * 16 + 16)
        tile = dot_nn(swap, sum_ref[tokens].reshape(256, 128)).astype(BF16)
        for c in range(COLS):
            out_ref[tokens, c * 128 : c * 128 + 128] = tile[c * 16 : c * 16 + 16]


def shape(dims, dtype):
    return jax.ShapeDtypeStruct(dims, dtype)


SMEM = pl.BlockSpec(memory_space=pltpu.SMEM)
WHOLE = pl.BlockSpec(memory_space=pltpu.VMEM)


def in_hbm(x):
    return pltpu.with_memory_space_constraint(x, pltpu.HBM)


def pack(half, query, key, value, decay, strength):
    return pl.pallas_call(
        pack_kernel,
        out_shape=shape((VALUE_HEADS, PACK_ROWS, 128), BF16),
        in_specs=[SMEM] + [pl.BlockSpec(memory_space=pltpu.HBM)] * 5,
        out_specs=WHOLE,
        scratch_shapes=[
            pltpu.VMEM((VALUE_HEADS, TOK), BF16),
            pltpu.VMEM((VALUE_HEADS, TOK), BF16),
            pltpu.SemaphoreType.DMA((4, VALUE_HEADS)),
        ],
        compiler_params=params(),
        name="pack",
    )(half, *(in_hbm(x) for x in (query, key, value, decay, strength)))


def route(ids, weights):
    return pl.pallas_call(
        route_kernel,
        out_shape=(
            shape((2, EXPERTS), jnp.int32),
            shape((TOK, 128), jnp.int32),
            shape((TOK, 128), F32),
        ),
        in_specs=[WHOLE, WHOLE],
        out_specs=(WHOLE, WHOLE, WHOLE),
        compiler_params=params(),
        name="route",
    )(ids, weights)


def mixer(received, weights):
    return pl.pallas_call(
        mixer_kernel,
        out_shape=(
            shape((BLOCKS, BLOCK, DH), BF16),
            pltpu.HBM((BLOCKS, BLOCK, DH), F32),
            pltpu.HBM((CHUNKS, MAP_ROWS, DH), F32),
            shape((CHUNKS, 8, DH), F32),
            shape((HALF_ROWS, DH), BF16),
        ),
        in_specs=[WHOLE] + [pl.BlockSpec(memory_space=pl.ANY)] * 3,
        out_specs=(WHOLE,) * 5,
        scratch_shapes=[
            pltpu.VMEM((BLOCKS, BLOCK, DH), BF16),
            pltpu.VMEM((BLOCKS, DH, BLOCK), F32),
            pltpu.VMEM((BLOCKS, BLOCK, DH), BF16),
            pltpu.VMEM((BLOCKS, 8, DH), F32),
        ],
        compiler_params=params(),
        name="mixer",
    )(received, *(in_hbm(w) for w in weights))


def compose(half, own, other):
    return pl.pallas_call(
        compose_kernel,
        out_shape=shape((SEG_ROWS, DH), BF16),
        in_specs=[SMEM, WHOLE, WHOLE],
        out_specs=WHOLE,
        compiler_params=params(),
        name="compose",
    )(half, own, other)


def fold(position, maps):
    return pl.pallas_call(
        fold_kernel,
        out_shape=shape((WIDTH, DH), F32),
        in_specs=[SMEM, WHOLE],
        out_specs=WHOLE,
        compiler_params=params(),
        name="fold",
    )(position, maps)


def head_rows(half, own, other, other_map, query_part, local, sub_map, sub_gain):
    return pl.pallas_call(
        head_kernel,
        out_shape=shape((BLOCKS, BLOCK, DH), BF16),
        in_specs=[SMEM] + [WHOLE] * 7,
        out_specs=WHOLE,
        scratch_shapes=[pltpu.VMEM((DH, DH), F32)],
        compiler_params=params(),
        name="heads",
    )(half, own, other, other_map, query_part, in_hbm(local), in_hbm(sub_map), sub_gain)


def mix(half, tok, heads, residual, out_gain, ffn_gain):
    return pl.pallas_call(
        mixed_kernel,
        out_shape=(shape((TOK, D), BF16), shape((SLOTS, 16, 128), BF16)),
        in_specs=[SMEM, SMEM] + [WHOLE] * 4,
        out_specs=(WHOLE, WHOLE),
        scratch_shapes=[pltpu.VMEM((TOK, 16, 128), BF16)],
        compiler_params=params(),
        name="mix",
    )(half, tok, heads, residual, out_gain, ffn_gain)


def experts(core, rows, weights):
    def place(which, step, core_ref):
        return (step, lax.rem(core_ref[0] + which, 2), 0, 0)

    block = pl.BlockSpec((FFN_ROWS // 2, 1, 32, 128), place)
    return pl.pallas_call(
        expert_kernel,
        grid_spec=pltpu.PrefetchScalarGridSpec(
            num_scalar_prefetch=1,
            grid=(2, EXPERTS // FFN_ROWS),
            in_specs=[block] + [pl.BlockSpec(w.shape, lambda *_: (0, 0)) for w in weights],
            out_specs=block,
            scratch_shapes=[pltpu.VMEM((FFN_ROWS, D), BF16)],
        ),
        out_shape=shape((CHIPS, 2, 32, 128), BF16),
        compiler_params=params(),
        name="experts",
    )(core, rows, *weights)


def combine(slots, weights, rows):
    return pl.pallas_call(
        combine_kernel,
        out_shape=shape((TOK, D), BF16),
        in_specs=[SMEM, SMEM, WHOLE],
        out_specs=WHOLE,
        scratch_shapes=[pltpu.VMEM((TOK, 16, 128), BF16)],
        compiler_params=params(),
        name="combine",
    )(slots, weights, rows)


def swap_all(x, axes):
    return lax.all_to_all(x, axes, split_axis=0, concat_axis=0, tiled=True)


def trade(x):
    return lax.ppermute(x, ("half", "pair"), [(0, 3), (3, 0), (1, 2), (2, 1)])


def neighbour(x):
    return lax.ppermute(x, "core", [(0, 1), (1, 0)])


HEAD_AXES = ("pair", "y")
SEQ_AXES = ("half", "pair", "y")
EXP_AXES = ("z", "core")
CHIP_AXES = SEQ_AXES + ("z",)


def body(
    mixer_query,
    mixer_key,
    mixer_value,
    log_decay,
    strength,
    residual,
    out_gain,
    ffn_gain,
    expert_ids,
    expert_weights,
    gate_proj,
    up_proj,
    down_proj,
):
    half = lax.axis_index("half").astype(jnp.int32).reshape(1)
    core = lax.axis_index("core").astype(jnp.int32).reshape(1)
    position = lax.axis_index(EXP_AXES).astype(jnp.int32).reshape(1)
    sent = pack(half, mixer_query[0], mixer_key[0], mixer_value[0], log_decay[0].T, strength[0].T)
    received = swap_all(sent, HEAD_AXES)
    tok, slots, weights = route(expert_ids[0], expert_weights[0])
    own = (gate_proj[0], up_proj[0], down_proj[0])
    other = tuple(neighbour(w) for w in own)
    query_part, local, sub_map, sub_gain, own_map = mixer(received, other)
    other_map = trade(own_map)
    maps = lax.all_gather(compose(half, own_map, other_map), EXP_AXES, axis=0)
    own_state = fold(position, maps)
    other_state = trade(own_state)
    outs = head_rows(half, own_state, other_state, other_map, query_part, local, sub_map, sub_gain)
    heads = swap_all(outs, HEAD_AXES)
    mixed, outgoing = mix(
        half, tok, heads, residual[0], out_gain.reshape(1, DH), ffn_gain.reshape(1, D)
    )
    arrived = swap_all(outgoing, CHIP_AXES)
    result = experts(core, arrived.reshape(CHIPS, 2, 32, 128), own + other)
    returned = swap_all(result.reshape(SLOTS, 16, 128), CHIP_AXES)
    ffn_out = combine(slots, weights, returned)
    return (mixed[None], ffn_out[None])


def solution(mesh):
    fine = Mesh(mesh.devices.reshape(2, 2, 8, 8, 2), SEQ_AXES + EXP_AXES)
    rows = P(EXP_AXES, SEQ_AXES, None)
    owned = P(SEQ_AXES + EXP_AXES, None, None)
    return jax.shard_map(
        body,
        mesh=fine,
        in_specs=(rows,) * 6 + (P(), P(), rows, rows) + (owned,) * 3,
        out_specs=(rows, rows),
        check_vma=False,
    )
```

```python
import jax
import jax.numpy as jnp
from jax import lax
from jax.experimental import pallas as pl
from jax.experimental.pallas import tpu as pltpu
from jax.sharding import Mesh
from jax.sharding import PartitionSpec as P

D = 2048
DH = 128
HK = 8
VALUE_HEADS = 16
TOPK = 10
BLOCK = 64
TOK = 64
EXPERTS = 512
WIDTH = 64
BLOCKS = 16
GROUP = 16
CHUNKS = 4
STEPS = 4
PACK_ROWS = 3 * TOK + 16
MAP_ROWS = 2 * DH
HALF_ROWS = MAP_ROWS + 32
SEG_ROWS = DH + WIDTH + 32
SLOTS = 2 * EXPERTS
COLS = D // 128
F32 = jnp.float32
BF16 = jnp.bfloat16
VMEM_LIMIT = 28 * 1024 * 1024


def params():
    return pltpu.CompilerParams(vmem_limit_bytes=VMEM_LIMIT)


def full(*arrays):
    return [pl.BlockSpec(memory_space=pltpu.VMEM) for _ in arrays]


def dot_nn(a, b):
    return lax.dot_general(a, b, (((1,), (0,)), ((), ())), preferred_element_type=F32)


def dot_nt(a, b):
    return lax.dot_general(a, b, (((1,), (1,)), ((), ())), preferred_element_type=F32)


def bdot_nn(a, b):
    return lax.dot_general(a, b, (((2,), (1,)), ((0,), (0,))), preferred_element_type=F32)


def bdot_nt(a, b):
    return lax.dot_general(a, b, (((2,), (2,)), ((0,), (0,))), preferred_element_type=F32)


def split(x):
    high = x.astype(BF16)
    return high, (x - high.astype(F32)).astype(BF16)


def swap_matrix():
    out_index = lax.broadcasted_iota(jnp.int32, (256, 256), 0)
    in_index = lax.broadcasted_iota(jnp.int32, (256, 256), 1)
    return (in_index == (out_index % 16) * 16 + out_index // 16).astype(BF16)


def pack_kernel(
    half_ref,
    query_ref,
    key_ref,
    value_ref,
    decay_ref,
    strength_ref,
    out_ref,
    decay_rows,
    strength_rows,
    sems,
):
    gate_copies = [
        pltpu.make_async_copy(decay_ref, decay_rows, sems.at[3, 0]),
        pltpu.make_async_copy(strength_ref, strength_rows, sems.at[3, 1]),
    ]
    copies = []
    for head in range(VALUE_HEADS):
        place = lax.rem(head + half_ref[0] * 8, VALUE_HEADS)
        for part, (ref, column) in enumerate(
            ((query_ref, head // 2), (key_ref, head // 2), (value_ref, head))
        ):
            copies.append(
                pltpu.make_async_copy(
                    ref.at[:, column * DH : column * DH + DH],
                    out_ref.at[place, part * TOK : part * TOK + TOK, :],
                    sems.at[part, head],
                )
            )
    for copy in gate_copies + copies:
        copy.start()
    for copy in gate_copies:
        copy.wait()
    gates = jnp.concatenate([decay_rows[...].astype(F32), strength_rows[...].astype(F32)], axis=1)
    for head in range(VALUE_HEADS):
        place = lax.rem(head + half_ref[0] * 8, VALUE_HEADS)
        out_ref[place, 192:208, :] = jnp.broadcast_to(gates[head : head + 1], (16, 128)).astype(BF16)
    for copy in copies:
        copy.wait()


def route_kernel(ids_ref, weight_in_ref, tok_ref, slot_ref, weight_ref):
    expert = lax.broadcasted_iota(jnp.int32, (TOK, EXPERTS), 1)
    named = jnp.zeros((TOK, EXPERTS), F32)
    for k in range(TOPK):
        named = jnp.where(ids_ref[:, k : k + 1] == expert, 1.0, named)
    row = lax.broadcasted_iota(jnp.int32, (TOK, TOK), 0)
    col = lax.broadcasted_iota(jnp.int32, (TOK, TOK), 1)
    rank = dot_nn((row > col).astype(BF16), named.astype(BF16))
    token = lax.broadcasted_iota(jnp.int32, (TOK, EXPERTS), 0).astype(F32)
    first = jnp.sum(jnp.where(rank == 0.0, token * named, 0.0), axis=0, keepdims=True)
    second = jnp.sum(jnp.where(rank == 1.0, token * named, 0.0), axis=0, keepdims=True)
    tok_ref[...] = jnp.concatenate([first, second], axis=0).astype(jnp.int32)
    lane = lax.broadcasted_iota(jnp.int32, (TOK, 128), 1)
    slots = jnp.zeros((TOK, 128), jnp.int32)
    weights = jnp.zeros((TOK, 128), F32)
    for k in range(TOPK):
        ids = ids_ref[:, k : k + 1]
        mine = jnp.sum(jnp.where(ids == expert, rank, 0.0), axis=1, keepdims=True)
        slots = jnp.where(lane == k, 2 * ids + mine.astype(jnp.int32), slots)
        weights = jnp.where(lane == k, weight_in_ref[:, k : k + 1], weights)
    slot_ref[:, 0:TOK] = jnp.transpose(slots.astype(F32))[0:16].astype(jnp.int32)
    slot_ref[:, TOK:128] = jnp.zeros((16, 128 - TOK), jnp.int32)
    weight_ref[:, 0:TOK] = jnp.transpose(weights)[0:16]
    weight_ref[:, TOK:128] = jnp.zeros((16, 128 - TOK), F32)


def spread_gain(gain):
    high, low = split(gain)
    rows = (16, DH)
    return (
        jnp.broadcast_to(high.astype(F32), rows).astype(BF16),
        jnp.broadcast_to(low.astype(F32), rows).astype(BF16),
    )


def read_gain(high, low):
    return (high.astype(F32) + low.astype(F32))[0:1]


def mixer_kernel(
    recv_ref,
    query_part_ref,
    local_ref,
    sub_map_ref,
    sub_gain_ref,
    send_ref,
    w_ref,
    u_ref,
    k_ref,
    gain_ref,
):
    row = lax.broadcasted_iota(jnp.int32, (BLOCK, BLOCK), 0)
    col = lax.broadcasted_iota(jnp.int32, (BLOCK, BLOCK), 1)
    eye = (row == col)[None]
    inclusive = (row >= col)[None]
    upper = (row <= col)[None]
    lower = (row > col)[None]

    def same(size):
        return ((row // size) == (col // size))[None]

    identity = jnp.broadcast_to(eye.astype(F32), (GROUP, BLOCK, BLOCK))
    wide_row = lax.broadcasted_iota(jnp.int32, (DH, DH), 0)
    wide_col = lax.broadcasted_iota(jnp.int32, (DH, DH), 1)
    wide_eye = jnp.broadcast_to((wide_row == wide_col).astype(F32)[None], (GROUP, DH, DH)).astype(BF16)

    def parts(step, unused):
        start = step * GROUP
        block = recv_ref[pl.ds(start, GROUP)]
        q = block[:, 0:64]
        k = block[:, 64:128]
        v = block[:, 128:192]
        gates = block[:, 192:208].astype(F32)
        decay_row = gates[:, 0:1, 0:64]
        strength_row = gates[:, 0:1, 64:128]
        qf = q.astype(F32)
        kf = k.astype(F32)
        q_norm = lax.rsqrt(jnp.sum(qf * qf, axis=2, keepdims=True) + 1e-06)
        k_norm = lax.rsqrt(jnp.sum(kf * kf, axis=2, keepdims=True) + 1e-06)
        k_norm_row = jnp.sum(jnp.where(eye, k_norm, 0.0), axis=1, keepdims=True)
        decay = jnp.sum(jnp.where(eye, decay_row, 0.0), axis=2, keepdims=True)
        strength = jnp.sum(jnp.where(eye, strength_row, 0.0), axis=2, keepdims=True)
        cum_row = jnp.sum(jnp.where(upper, decay, 0.0), axis=1, keepdims=True)
        cum = jnp.sum(jnp.where(inclusive, decay_row, 0.0), axis=2, keepdims=True)
        spread = cum - cum_row
        fade = jnp.where(inclusive, jnp.exp(jnp.where(inclusive, spread, 0.0)), 0.0)
        key_dot = bdot_nt(k, k) * (k_norm * k_norm_row)
        query_dot = bdot_nt(q, k) * (q_norm * k_norm_row)
        negated = jnp.where(lower, -(strength * key_dot * fade), 0.0)
        inverse = identity + jnp.where(same(2), negated, 0.0)
        for size in (2, 4, 8, 16, 32):
            cross = jnp.where(same(2 * size) & ~same(size), negated, 0.0).astype(BF16)
            half = inverse.astype(BF16)
            inverse = inverse + bdot_nn(bdot_nn(half, cross).astype(BF16), half)
        inverse_half = inverse.astype(BF16)
        decay_gain = jnp.exp(cum)
        last = cum[:, BLOCK - 1 : BLOCK, :]
        tail = jnp.exp(last - cum)
        unit_k = k_norm * kf
        w = bdot_nn(inverse_half, ((strength * decay_gain) * unit_k).astype(BF16)).astype(BF16)
        v_t = bdot_nt(wide_eye, v) * strength_row
        u_t = bdot_nt(v_t.astype(BF16), inverse_half)
        scores = (query_dot * fade).astype(BF16)
        q_part = decay_gain * (q_norm * qf) - bdot_nn(scores, w)
        local = bdot_nt(scores, u_t.astype(BF16))
        w_ref[pl.ds(start, GROUP)] = w
        u_ref[pl.ds(start, GROUP)] = u_t
        k_ref[pl.ds(start, GROUP)] = (tail * unit_k).astype(BF16)
        gain_ref[pl.ds(start, GROUP)] = jnp.broadcast_to(jnp.exp(last), (GROUP, 8, 128))
        query_part_ref[pl.ds(start, GROUP)] = q_part.astype(BF16)
        local_ref[pl.ds(start, GROUP)] = local
        return unused

    lax.fori_loop(0, BLOCKS // GROUP, parts, 0)

    map_row = lax.broadcasted_iota(jnp.int32, (MAP_ROWS, DH), 0)
    map_col = lax.broadcasted_iota(jnp.int32, (MAP_ROWS, DH), 1)
    diagonal = map_row == map_col
    start_map = jnp.where(diagonal, 1.0, 0.0).astype(F32)

    def advance(step, carried):
        maps, gains = carried
        new_maps, new_gains = [], []
        for chunk in range(CHUNKS):
            index = chunk * STEPS + step
            state = maps[chunk]
            half = state.astype(BF16)
            out = dot_nt(query_part_ref[index], half)
            seen = dot_nt(half, w_ref[index])
            fresh = jnp.concatenate([-seen[0:DH], u_ref[index] - seen[DH:MAP_ROWS]], axis=0)
            gain = gain_ref[index][0:1, :]
            query_part_ref[index] = out[:, 0:DH].astype(BF16)
            local_ref[index] = local_ref[index] + out[:, DH:MAP_ROWS]
            new_maps.append(gain * state + dot_nn(fresh.astype(BF16), k_ref[index]))
            new_gains.append(gain * gains[chunk])
        return tuple(new_maps), tuple(new_gains)

    maps, gains = lax.fori_loop(
        0,
        STEPS,
        advance,
        (
            tuple(start_map for _ in range(CHUNKS)),
            tuple(jnp.ones((1, DH), F32) for _ in range(CHUNKS)),
        ),
    )
    whole = None
    for chunk in range(CHUNKS):
        gain = gains[chunk]
        changed = maps[chunk] - jnp.where(diagonal, gain, 0.0)
        sub_map_ref[chunk] = changed
        sub_gain_ref[chunk] = jnp.broadcast_to(gain, (8, DH))
        if whole is None:
            whole, total = maps[chunk], gain
        else:
            added = jnp.where(map_row < DH, 0.0, changed)
            whole = gain * whole + dot_nn(whole.astype(BF16), changed[0:DH].astype(BF16)) + added
            total = gain * total
    send_ref[0:MAP_ROWS, :] = (whole - jnp.where(diagonal, total, 0.0)).astype(BF16)
    high, low = spread_gain(total)
    send_ref[MAP_ROWS : MAP_ROWS + 16, :] = high
    send_ref[MAP_ROWS + 16 : MAP_ROWS + 32, :] = low


def compose_kernel(half_ref, own_ref, other_ref, out_ref):
    map_row = lax.broadcasted_iota(jnp.int32, (MAP_ROWS, DH), 0)
    map_col = lax.broadcasted_iota(jnp.int32, (MAP_ROWS, DH), 1)
    diagonal = map_row == map_col

    def emit(first_ref, second_ref, start):
        gain_first = read_gain(first_ref[MAP_ROWS : MAP_ROWS + 16], first_ref[MAP_ROWS + 16 : MAP_ROWS + 32])
        gain = read_gain(second_ref[MAP_ROWS : MAP_ROWS + 16], second_ref[MAP_ROWS + 16 : MAP_ROWS + 32])
        total = gain * gain_first
        first = first_ref[0:MAP_ROWS, :].astype(F32) + jnp.where(diagonal, gain_first, 0.0)
        second = second_ref[0:MAP_ROWS, :].astype(F32)
        whole = gain * first + dot_nn(first.astype(BF16), second_ref[0:DH, :])
        whole = whole + jnp.where(map_row < DH, 0.0, second) - jnp.where(diagonal, total, 0.0)
        out_ref[0:DH, :] = whole[0:DH].astype(BF16)
        out_ref[DH : DH + WIDTH, :] = whole[DH + start : DH + start + WIDTH].astype(BF16)
        high, low = spread_gain(total)
        out_ref[DH + WIDTH : DH + WIDTH + 16, :] = high
        out_ref[DH + WIDTH + 16 : DH + WIDTH + 32, :] = low

    @pl.when(half_ref[0] == 0)
    def _():
        emit(own_ref, other_ref, 0)

    @pl.when(half_ref[0] != 0)
    def _():
        emit(other_ref, own_ref, WIDTH)


def fold_kernel(position_ref, maps_ref, out_ref):
    def fold(index, state):
        gain = read_gain(
            maps_ref[index, DH + WIDTH : DH + WIDTH + 16, :],
            maps_ref[index, DH + WIDTH + 16 : DH + WIDTH + 32, :],
        )
        return (
            gain * state
            + dot_nn(state.astype(BF16), maps_ref[index, 0:DH, :])
            + maps_ref[index, DH : DH + WIDTH, :].astype(F32)
        )

    out_ref[...] = lax.fori_loop(0, position_ref[0], fold, jnp.zeros((WIDTH, DH), F32))


def head_kernel(
    half_ref,
    own_ref,
    other_ref,
    other_map_ref,
    query_part_ref,
    local_ref,
    sub_map_ref,
    sub_gain_ref,
    out_ref,
    state_ref,
):
    @pl.when(half_ref[0] == 0)
    def _():
        state_ref[0:WIDTH, :] = own_ref[...]
        state_ref[WIDTH:DH, :] = other_ref[...]

    @pl.when(half_ref[0] != 0)
    def _():
        state = jnp.concatenate([other_ref[...], own_ref[...]], axis=0)
        gain = read_gain(
            other_map_ref[MAP_ROWS : MAP_ROWS + 16, :], other_map_ref[MAP_ROWS + 16 : MAP_ROWS + 32, :]
        )
        state_ref[...] = (
            gain * state
            + dot_nn(state.astype(BF16), other_map_ref[0:DH, :])
            + other_map_ref[DH:MAP_ROWS, :].astype(F32)
        )

    state = state_ref[...]
    for chunk in range(CHUNKS):
        half = state.astype(BF16)
        for step in range(STEPS):
            index = chunk * STEPS + step
            out_ref[index] = (dot_nt(query_part_ref[index], half) + local_ref[index]).astype(BF16)
        if chunk + 1 < CHUNKS:
            changed = sub_map_ref[chunk]
            state = (
                sub_gain_ref[chunk][0:1] * state
                + dot_nn(half, changed[0:DH].astype(BF16))
                + changed[DH:MAP_ROWS]
            )


def mixed_kernel(
    half_ref,
    tok_ref,
    heads_ref,
    residual_ref,
    out_gain_ref,
    ffn_gain_ref,
    mixed_ref,
    send_ref,
    rows_ref,
):
    gain = out_gain_ref[...]
    total = jnp.zeros((TOK, 1), F32)
    for head in range(VALUE_HEADS):
        wide = heads_ref[lax.rem(head + half_ref[0] * 8, VALUE_HEADS)].astype(F32)
        scale = lax.rsqrt(jnp.mean(wide * wide, axis=1, keepdims=True) + 1e-06)
        part = slice(head * DH, head * DH + DH)
        mixed = (residual_ref[:, part].astype(F32) + wide * scale * gain).astype(BF16)
        mixed_ref[:, part] = mixed
        mixed_wide = mixed.astype(F32)
        total = total + jnp.sum(mixed_wide * mixed_wide, axis=1, keepdims=True)
    scale = lax.rsqrt(total * (1.0 / D) + 1e-06)
    swap = swap_matrix()
    for group in range(TOK // 16):
        tokens = slice(group * 16, group * 16 + 16)
        pieces = []
        for c in range(COLS):
            part = slice(c * 128, c * 128 + 128)
            value = mixed_ref[tokens, part].astype(F32) * scale[tokens] * ffn_gain_ref[:, part]
            pieces.append(value.astype(BF16))
        swapped = dot_nn(swap, jnp.concatenate(pieces, axis=0)).astype(BF16)
        rows_ref[tokens] = swapped.reshape(16, 16, 128)

    def place(expert, unused):
        send_ref[2 * expert] = rows_ref[tok_ref[expert]]
        send_ref[2 * expert + 1] = rows_ref[tok_ref[EXPERTS + expert]]
        return unused

    lax.fori_loop(0, EXPERTS, place, 0, unroll=16)


FFN_ROWS = 256


def expert_kernel(rows_ref, gate_ref, up_ref, down_ref, out_ref, wide_ref):
    swap = swap_matrix()
    for pair in range(FFN_ROWS // 32):
        start = pair * 512
        rows = [rows_ref[start : start + 256, :], rows_ref[start + 256 : start + 512, :]]
        tile = dot_nn(swap, jnp.concatenate(rows, axis=1)).astype(BF16)
        for c in range(COLS):
            part = slice(c * 128, c * 128 + 128)
            wide_ref[pair * 32 : pair * 32 + 16, part] = tile[c * 16 : c * 16 + 16, 0:128]
            wide_ref[pair * 32 + 16 : pair * 32 + 32, part] = tile[c * 16 : c * 16 + 16, 128:256]
    wide = wide_ref[...]
    gate = dot_nn(wide, gate_ref[...])
    up = dot_nn(wide, up_ref[...])
    hidden = (gate / (1.0 + jnp.exp(-gate)) * up).astype(BF16)
    wide_ref[...] = dot_nn(hidden, down_ref[...]).astype(BF16)
    for pair in range(FFN_ROWS // 32):
        sides = []
        for start in (pair * 32, pair * 32 + 16):
            pieces = [wide_ref[start : start + 16, c * 128 : c * 128 + 128] for c in range(COLS)]
            sides.append(jnp.concatenate(pieces, axis=0))
        tile = dot_nn(swap, jnp.concatenate(sides, axis=1)).astype(BF16)
        out_ref[pair * 512 : pair * 512 + 256, :] = tile[:, 0:128]
        out_ref[pair * 512 + 256 : pair * 512 + 512, :] = tile[:, 128:256]


def combine_kernel(slot_ref, weight_ref, rows_ref, out_ref, sum_ref):
    def token(index, unused):
        total = jnp.zeros((16, 128), F32)
        for k in range(TOPK):
            place = k * 128 + index
            total = total + weight_ref[place] * rows_ref[slot_ref[place]].astype(F32)
        sum_ref[index] = total.astype(BF16)
        return unused

    lax.fori_loop(0, TOK, token, 0, unroll=4)
    swap = swap_matrix()
    for group in range(TOK // 16):
        tokens = slice(group * 16, group * 16 + 16)
        tile = dot_nn(swap, sum_ref[tokens].reshape(256, 128)).astype(BF16)
        for c in range(COLS):
            out_ref[tokens, c * 128 : c * 128 + 128] = tile[c * 16 : c * 16 + 16]


def shape(dims, dtype):
    return jax.ShapeDtypeStruct(dims, dtype)


SMEM = pl.BlockSpec(memory_space=pltpu.SMEM)
WHOLE = pl.BlockSpec(memory_space=pltpu.VMEM)


def in_hbm(x):
    return pltpu.with_memory_space_constraint(x, pltpu.HBM)


def pack(half, query, key, value, decay, strength):
    return pl.pallas_call(
        pack_kernel,
        out_shape=shape((VALUE_HEADS, PACK_ROWS, 128), BF16),
        in_specs=[SMEM] + [pl.BlockSpec(memory_space=pltpu.HBM)] * 5,
        out_specs=WHOLE,
        scratch_shapes=[
            pltpu.VMEM((VALUE_HEADS, TOK), BF16),
            pltpu.VMEM((VALUE_HEADS, TOK), BF16),
            pltpu.SemaphoreType.DMA((4, VALUE_HEADS)),
        ],
        compiler_params=params(),
        name="pack",
    )(half, *(in_hbm(x) for x in (query, key, value, decay, strength)))


def route(ids, weights):
    return pl.pallas_call(
        route_kernel,
        out_shape=(
            shape((2, EXPERTS), jnp.int32),
            shape((16, 128), jnp.int32),
            shape((16, 128), F32),
        ),
        in_specs=[WHOLE, WHOLE],
        out_specs=(WHOLE, WHOLE, WHOLE),
        compiler_params=params(),
        name="route",
    )(ids, weights)


def mixer(received):
    return pl.pallas_call(
        mixer_kernel,
        out_shape=(
            shape((BLOCKS, BLOCK, DH), BF16),
            shape((BLOCKS, BLOCK, DH), F32),
            shape((CHUNKS, MAP_ROWS, DH), F32),
            shape((CHUNKS, 8, DH), F32),
            shape((HALF_ROWS, DH), BF16),
        ),
        in_specs=[WHOLE],
        out_specs=(WHOLE,) * 5,
        scratch_shapes=[
            pltpu.VMEM((BLOCKS, BLOCK, DH), BF16),
            pltpu.VMEM((BLOCKS, DH, BLOCK), F32),
            pltpu.VMEM((BLOCKS, BLOCK, DH), BF16),
            pltpu.VMEM((BLOCKS, 8, DH), F32),
        ],
        compiler_params=params(),
        name="mixer",
    )(received)


def compose(half, own, other):
    return pl.pallas_call(
        compose_kernel,
        out_shape=shape((SEG_ROWS, DH), BF16),
        in_specs=[SMEM, WHOLE, WHOLE],
        out_specs=WHOLE,
        compiler_params=params(),
        name="compose",
    )(half, own, other)


def fold(position, maps):
    return pl.pallas_call(
        fold_kernel,
        out_shape=shape((WIDTH, DH), F32),
        in_specs=[SMEM, WHOLE],
        out_specs=WHOLE,
        compiler_params=params(),
        name="fold",
    )(position, maps)


def head_rows(half, own, other, other_map, query_part, local, sub_map, sub_gain):
    return pl.pallas_call(
        head_kernel,
        out_shape=shape((BLOCKS, BLOCK, DH), BF16),
        in_specs=[SMEM] + [WHOLE] * 7,
        out_specs=WHOLE,
        scratch_shapes=[pltpu.VMEM((DH, DH), F32)],
        compiler_params=params(),
        name="heads",
    )(half, own, other, other_map, query_part, local, sub_map, sub_gain)


def mix(half, tok, heads, residual, out_gain, ffn_gain):
    return pl.pallas_call(
        mixed_kernel,
        out_shape=(shape((TOK, D), BF16), shape((SLOTS, 16, 128), BF16)),
        in_specs=[SMEM, SMEM] + [WHOLE] * 4,
        out_specs=(WHOLE, WHOLE),
        scratch_shapes=[pltpu.VMEM((TOK, 16, 128), BF16)],
        compiler_params=params(),
        name="mix",
    )(half, tok.reshape(SLOTS), heads, residual, out_gain, ffn_gain)


def experts(rows, gate, up, down):
    hidden = gate.shape[1]
    block = pl.BlockSpec((FFN_ROWS * 16, 128), lambda i: (i, 0))
    return pl.pallas_call(
        expert_kernel,
        grid=(SLOTS // FFN_ROWS,),
        out_shape=shape((SLOTS * 16, 128), BF16),
        in_specs=[
            block,
            pl.BlockSpec((D, hidden), lambda i: (0, 0)),
            pl.BlockSpec((D, hidden), lambda i: (0, 0)),
            pl.BlockSpec((hidden, D), lambda i: (0, 0)),
        ],
        out_specs=block,
        scratch_shapes=[pltpu.VMEM((FFN_ROWS, D), BF16)],
        compiler_params=params(),
        name="experts",
    )(rows, gate, up, down)


def combine(slots, weights, rows):
    return pl.pallas_call(
        combine_kernel,
        out_shape=shape((TOK, D), BF16),
        in_specs=[SMEM, SMEM, WHOLE],
        out_specs=WHOLE,
        scratch_shapes=[pltpu.VMEM((TOK, 16, 128), BF16)],
        compiler_params=params(),
        name="combine",
    )(slots.reshape(16 * 128), weights.reshape(16 * 128), rows)


def swap_all(x, axes):
    return lax.all_to_all(x, axes, split_axis=0, concat_axis=0, tiled=True)


def trade(x):
    return lax.ppermute(x, ("half", "pair"), [(0, 3), (3, 0), (1, 2), (2, 1)])


HEAD_AXES = ("pair", "y")
SEQ_AXES = ("half", "pair", "y")
EXP_AXES = ("z", "core")


def body(
    mixer_query,
    mixer_key,
    mixer_value,
    log_decay,
    strength,
    residual,
    out_gain,
    ffn_gain,
    expert_ids,
    expert_weights,
    gate_proj,
    up_proj,
    down_proj,
):
    half = lax.axis_index("half").astype(jnp.int32).reshape(1)
    position = lax.axis_index(EXP_AXES).astype(jnp.int32).reshape(1)
    sent = pack(half, mixer_query[0], mixer_key[0], mixer_value[0], log_decay[0].T, strength[0].T)
    received = swap_all(sent, HEAD_AXES)
    tok, slots, weights = route(expert_ids[0], expert_weights[0])
    query_part, local, sub_map, sub_gain, own_map = mixer(received)
    other_map = trade(own_map)
    maps = lax.all_gather(compose(half, own_map, other_map), EXP_AXES, axis=0)
    own_state = fold(position, maps)
    other_state = trade(own_state)
    outs = head_rows(half, own_state, other_state, other_map, query_part, local, sub_map, sub_gain)
    heads = swap_all(outs, HEAD_AXES)
    mixed, outgoing = mix(
        half, tok, heads, residual[0], out_gain.reshape(1, DH), ffn_gain.reshape(1, D)
    )
    arrived = swap_all(outgoing, SEQ_AXES + EXP_AXES)
    result = experts(arrived.reshape(SLOTS * 16, 128), gate_proj[0], up_proj[0], down_proj[0])
    returned = swap_all(result.reshape(SLOTS, 16, 128), SEQ_AXES + EXP_AXES)
    ffn_out = combine(slots, weights, returned)
    return (mixed[None], ffn_out[None])


def solution(mesh):
    fine = Mesh(mesh.devices.reshape(2, 2, 8, 8, 2), SEQ_AXES + EXP_AXES)
    rows = P(EXP_AXES, SEQ_AXES, None)
    owned = P(SEQ_AXES + EXP_AXES, None, None)
    return jax.shard_map(
        body,
        mesh=fine,
        in_specs=(rows,) * 6 + (P(), P(), rows, rows) + (owned,) * 3,
        out_specs=(rows, rows),
        check_vma=False,
    )
```

```python
import jax
import jax.numpy as jnp
from jax import lax
from jax.experimental import pallas as pl
from jax.experimental.pallas import tpu as pltpu
from jax.sharding import Mesh
from jax.sharding import PartitionSpec as P

D = 2048
DH = 128
HK = 8
VALUE_HEADS = 16
TOPK = 10
BLOCK = 64
TOK = 64
EXPERTS = 512
WIDTH = 64
BLOCKS = 16
GROUP = 16
CHUNKS = 4
STEPS = 4
PACK_ROWS = 3 * TOK + 16
MAP_ROWS = 2 * DH
HALF_ROWS = MAP_ROWS + 32
SEG_ROWS = DH + WIDTH + 32
SLOTS = 2 * EXPERTS
COLS = D // 128
F32 = jnp.float32
BF16 = jnp.bfloat16
VMEM_LIMIT = 28 * 1024 * 1024


def params():
    return pltpu.CompilerParams(vmem_limit_bytes=VMEM_LIMIT)


def full(*arrays):
    return [pl.BlockSpec(memory_space=pltpu.VMEM) for _ in arrays]


def dot_nn(a, b):
    return lax.dot_general(a, b, (((1,), (0,)), ((), ())), preferred_element_type=F32)


def dot_nt(a, b):
    return lax.dot_general(a, b, (((1,), (1,)), ((), ())), preferred_element_type=F32)


def bdot_nn(a, b):
    return lax.dot_general(a, b, (((2,), (1,)), ((0,), (0,))), preferred_element_type=F32)


def bdot_nt(a, b):
    return lax.dot_general(a, b, (((2,), (2,)), ((0,), (0,))), preferred_element_type=F32)


def split(x):
    high = x.astype(BF16)
    return high, (x - high.astype(F32)).astype(BF16)


def swap_matrix():
    out_index = lax.broadcasted_iota(jnp.int32, (256, 256), 0)
    in_index = lax.broadcasted_iota(jnp.int32, (256, 256), 1)
    return (in_index == (out_index % 16) * 16 + out_index // 16).astype(BF16)


def pack_kernel(
    half_ref,
    query_ref,
    key_ref,
    value_ref,
    decay_ref,
    strength_ref,
    out_ref,
    decay_rows,
    strength_rows,
    sems,
):
    gate_copies = [
        pltpu.make_async_copy(decay_ref, decay_rows, sems.at[3, 0]),
        pltpu.make_async_copy(strength_ref, strength_rows, sems.at[3, 1]),
    ]
    copies = []
    for head in range(VALUE_HEADS):
        place = lax.rem(head + half_ref[0] * 8, VALUE_HEADS)
        for part, (ref, column) in enumerate(
            ((query_ref, head // 2), (key_ref, head // 2), (value_ref, head))
        ):
            copies.append(
                pltpu.make_async_copy(
                    ref.at[:, column * DH : column * DH + DH],
                    out_ref.at[place, part * TOK : part * TOK + TOK, :],
                    sems.at[part, head],
                )
            )
    for copy in gate_copies + copies:
        copy.start()
    for copy in gate_copies:
        copy.wait()
    gates = jnp.concatenate([decay_rows[...].astype(F32), strength_rows[...].astype(F32)], axis=1)
    for head in range(VALUE_HEADS):
        place = lax.rem(head + half_ref[0] * 8, VALUE_HEADS)
        out_ref[place, 192:208, :] = jnp.broadcast_to(gates[head : head + 1], (16, 128)).astype(BF16)
    for copy in copies:
        copy.wait()


Y_AXES = ("y4", "y2", "y1")
HEAD_AXES = ("pair",) + Y_AXES
SEQ_AXES = ("half",) + HEAD_AXES
EXP_AXES = ("z4", "z2", "z1", "core")
ROW_AXES = ("core", "half", "pair", "y1", "z1", "y2", "z2", "y4", "z4")
OWNER_AXES = SEQ_AXES + EXP_AXES


def reorder_bits(index, old, new):
    moved = jnp.zeros_like(index)
    for place, axis in enumerate(reversed(new)):
        bit = (index >> (len(old) - 1 - old.index(axis))) & 1
        moved = moved | (bit << place)
    return moved


def route_kernel(ids_ref, weight_in_ref, tok_ref, slot_ref, weight_ref):
    expert = reorder_bits(
        lax.broadcasted_iota(jnp.int32, (TOK, EXPERTS), 1), ROW_AXES, OWNER_AXES
    )
    named = jnp.zeros((TOK, EXPERTS), F32)
    for k in range(TOPK):
        named = jnp.where(ids_ref[:, k : k + 1] == expert, 1.0, named)
    row = lax.broadcasted_iota(jnp.int32, (TOK, TOK), 0)
    col = lax.broadcasted_iota(jnp.int32, (TOK, TOK), 1)
    rank = dot_nn((row > col).astype(BF16), named.astype(BF16))
    token = lax.broadcasted_iota(jnp.int32, (TOK, EXPERTS), 0).astype(F32)
    first = jnp.sum(jnp.where(rank == 0.0, token * named, 0.0), axis=0, keepdims=True)
    second = jnp.sum(jnp.where(rank == 1.0, token * named, 0.0), axis=0, keepdims=True)
    tok_ref[...] = jnp.concatenate([first, second], axis=0).astype(jnp.int32)
    lane = lax.broadcasted_iota(jnp.int32, (TOK, 128), 1)
    slots = jnp.zeros((TOK, 128), jnp.int32)
    weights = jnp.zeros((TOK, 128), F32)
    for k in range(TOPK):
        ids = ids_ref[:, k : k + 1]
        mine = jnp.sum(jnp.where(ids == expert, rank, 0.0), axis=1, keepdims=True)
        place = reorder_bits(ids, OWNER_AXES, ROW_AXES)
        slots = jnp.where(lane == k, 2 * place + mine.astype(jnp.int32), slots)
        weights = jnp.where(lane == k, weight_in_ref[:, k : k + 1], weights)
    slot_ref[:, 0:TOK] = jnp.transpose(slots.astype(F32))[0:16].astype(jnp.int32)
    slot_ref[:, TOK:128] = jnp.zeros((16, 128 - TOK), jnp.int32)
    weight_ref[:, 0:TOK] = jnp.transpose(weights)[0:16]
    weight_ref[:, TOK:128] = jnp.zeros((16, 128 - TOK), F32)


def spread_gain(gain):
    high, low = split(gain)
    rows = (16, DH)
    return (
        jnp.broadcast_to(high.astype(F32), rows).astype(BF16),
        jnp.broadcast_to(low.astype(F32), rows).astype(BF16),
    )


def read_gain(high, low):
    return (high.astype(F32) + low.astype(F32))[0:1]


def mixer_kernel(
    recv_ref,
    query_part_ref,
    local_ref,
    sub_map_ref,
    sub_gain_ref,
    send_ref,
    w_ref,
    u_ref,
    k_ref,
    gain_ref,
):
    row = lax.broadcasted_iota(jnp.int32, (BLOCK, BLOCK), 0)
    col = lax.broadcasted_iota(jnp.int32, (BLOCK, BLOCK), 1)
    eye = (row == col)[None]
    inclusive = (row >= col)[None]
    upper = (row <= col)[None]
    lower = (row > col)[None]

    def same(size):
        return ((row // size) == (col // size))[None]

    identity = jnp.broadcast_to(eye.astype(F32), (GROUP, BLOCK, BLOCK))
    wide_row = lax.broadcasted_iota(jnp.int32, (DH, DH), 0)
    wide_col = lax.broadcasted_iota(jnp.int32, (DH, DH), 1)
    wide_eye = jnp.broadcast_to((wide_row == wide_col).astype(F32)[None], (GROUP, DH, DH)).astype(BF16)

    def parts(step, unused):
        start = step * GROUP
        block = recv_ref[pl.ds(start, GROUP)]
        q = block[:, 0:64]
        k = block[:, 64:128]
        v = block[:, 128:192]
        gates = block[:, 192:208].astype(F32)
        decay_row = gates[:, 0:1, 0:64]
        strength_row = gates[:, 0:1, 64:128]
        qf = q.astype(F32)
        kf = k.astype(F32)
        q_norm = lax.rsqrt(jnp.sum(qf * qf, axis=2, keepdims=True) + 1e-06)
        k_norm = lax.rsqrt(jnp.sum(kf * kf, axis=2, keepdims=True) + 1e-06)
        k_norm_row = jnp.sum(jnp.where(eye, k_norm, 0.0), axis=1, keepdims=True)
        decay = jnp.sum(jnp.where(eye, decay_row, 0.0), axis=2, keepdims=True)
        strength = jnp.sum(jnp.where(eye, strength_row, 0.0), axis=2, keepdims=True)
        cum_row = jnp.sum(jnp.where(upper, decay, 0.0), axis=1, keepdims=True)
        cum = jnp.sum(jnp.where(inclusive, decay_row, 0.0), axis=2, keepdims=True)
        spread = cum - cum_row
        fade = jnp.where(inclusive, jnp.exp(jnp.where(inclusive, spread, 0.0)), 0.0)
        key_dot = bdot_nt(k, k) * (k_norm * k_norm_row)
        query_dot = bdot_nt(q, k) * (q_norm * k_norm_row)
        negated = jnp.where(lower, -(strength * key_dot * fade), 0.0)
        inverse = identity + jnp.where(same(2), negated, 0.0)
        for size in (2, 4, 8, 16, 32):
            cross = jnp.where(same(2 * size) & ~same(size), negated, 0.0).astype(BF16)
            half = inverse.astype(BF16)
            inverse = inverse + bdot_nn(bdot_nn(half, cross).astype(BF16), half)
        inverse_half = inverse.astype(BF16)
        decay_gain = jnp.exp(cum)
        last = cum[:, BLOCK - 1 : BLOCK, :]
        tail = jnp.exp(last - cum)
        unit_k = k_norm * kf
        w = bdot_nn(inverse_half, ((strength * decay_gain) * unit_k).astype(BF16)).astype(BF16)
        v_t = bdot_nt(wide_eye, v) * strength_row
        u_t = bdot_nt(v_t.astype(BF16), inverse_half)
        scores = (query_dot * fade).astype(BF16)
        q_part = decay_gain * (q_norm * qf) - bdot_nn(scores, w)
        local = bdot_nt(scores, u_t.astype(BF16))
        w_ref[pl.ds(start, GROUP)] = w
        u_ref[pl.ds(start, GROUP)] = u_t
        k_ref[pl.ds(start, GROUP)] = (tail * unit_k).astype(BF16)
        gain_ref[pl.ds(start, GROUP)] = jnp.broadcast_to(jnp.exp(last), (GROUP, 8, 128))
        query_part_ref[pl.ds(start, GROUP)] = q_part.astype(BF16)
        local_ref[pl.ds(start, GROUP)] = local
        return unused

    lax.fori_loop(0, BLOCKS // GROUP, parts, 0)

    map_row = lax.broadcasted_iota(jnp.int32, (MAP_ROWS, DH), 0)
    map_col = lax.broadcasted_iota(jnp.int32, (MAP_ROWS, DH), 1)
    diagonal = map_row == map_col
    start_map = jnp.where(diagonal, 1.0, 0.0).astype(F32)

    def advance(step, carried):
        maps, gains = carried
        new_maps, new_gains = [], []
        for chunk in range(CHUNKS):
            index = chunk * STEPS + step
            state = maps[chunk]
            half = state.astype(BF16)
            out = dot_nt(query_part_ref[index], half)
            seen = dot_nt(half, w_ref[index])
            fresh = jnp.concatenate([-seen[0:DH], u_ref[index] - seen[DH:MAP_ROWS]], axis=0)
            gain = gain_ref[index][0:1, :]
            query_part_ref[index] = out[:, 0:DH].astype(BF16)
            local_ref[index] = local_ref[index] + out[:, DH:MAP_ROWS]
            new_maps.append(gain * state + dot_nn(fresh.astype(BF16), k_ref[index]))
            new_gains.append(gain * gains[chunk])
        return tuple(new_maps), tuple(new_gains)

    maps, gains = lax.fori_loop(
        0,
        STEPS,
        advance,
        (
            tuple(start_map for _ in range(CHUNKS)),
            tuple(jnp.ones((1, DH), F32) for _ in range(CHUNKS)),
        ),
    )
    whole = None
    for chunk in range(CHUNKS):
        gain = gains[chunk]
        changed = maps[chunk] - jnp.where(diagonal, gain, 0.0)
        sub_map_ref[chunk] = changed
        sub_gain_ref[chunk] = jnp.broadcast_to(gain, (8, DH))
        if whole is None:
            whole, total = maps[chunk], gain
        else:
            added = jnp.where(map_row < DH, 0.0, changed)
            whole = gain * whole + dot_nn(whole.astype(BF16), changed[0:DH].astype(BF16)) + added
            total = gain * total
    send_ref[0:MAP_ROWS, :] = (whole - jnp.where(diagonal, total, 0.0)).astype(BF16)
    high, low = spread_gain(total)
    send_ref[MAP_ROWS : MAP_ROWS + 16, :] = high
    send_ref[MAP_ROWS + 16 : MAP_ROWS + 32, :] = low


def compose_kernel(half_ref, own_ref, other_ref, out_ref):
    map_row = lax.broadcasted_iota(jnp.int32, (MAP_ROWS, DH), 0)
    map_col = lax.broadcasted_iota(jnp.int32, (MAP_ROWS, DH), 1)
    diagonal = map_row == map_col

    def emit(first_ref, second_ref, start):
        gain_first = read_gain(first_ref[MAP_ROWS : MAP_ROWS + 16], first_ref[MAP_ROWS + 16 : MAP_ROWS + 32])
        gain = read_gain(second_ref[MAP_ROWS : MAP_ROWS + 16], second_ref[MAP_ROWS + 16 : MAP_ROWS + 32])
        total = gain * gain_first
        first = first_ref[0:MAP_ROWS, :].astype(F32) + jnp.where(diagonal, gain_first, 0.0)
        second = second_ref[0:MAP_ROWS, :].astype(F32)
        whole = gain * first + dot_nn(first.astype(BF16), second_ref[0:DH, :])
        whole = whole + jnp.where(map_row < DH, 0.0, second) - jnp.where(diagonal, total, 0.0)
        out_ref[0:DH, :] = whole[0:DH].astype(BF16)
        out_ref[DH : DH + WIDTH, :] = whole[DH + start : DH + start + WIDTH].astype(BF16)
        high, low = spread_gain(total)
        out_ref[DH + WIDTH : DH + WIDTH + 16, :] = high
        out_ref[DH + WIDTH + 16 : DH + WIDTH + 32, :] = low

    @pl.when(half_ref[0] == 0)
    def _():
        emit(own_ref, other_ref, 0)

    @pl.when(half_ref[0] != 0)
    def _():
        emit(other_ref, own_ref, WIDTH)


def fold_kernel(position_ref, maps_ref, out_ref):
    def fold(index, state):
        gain = read_gain(
            maps_ref[index, DH + WIDTH : DH + WIDTH + 16, :],
            maps_ref[index, DH + WIDTH + 16 : DH + WIDTH + 32, :],
        )
        return (
            gain * state
            + dot_nn(state.astype(BF16), maps_ref[index, 0:DH, :])
            + maps_ref[index, DH : DH + WIDTH, :].astype(F32)
        )

    out_ref[...] = lax.fori_loop(0, position_ref[0], fold, jnp.zeros((WIDTH, DH), F32))


def head_kernel(
    half_ref,
    own_ref,
    other_ref,
    other_map_ref,
    query_part_ref,
    local_ref,
    sub_map_ref,
    sub_gain_ref,
    out_ref,
    state_ref,
):
    @pl.when(half_ref[0] == 0)
    def _():
        state_ref[0:WIDTH, :] = own_ref[...]
        state_ref[WIDTH:DH, :] = other_ref[...]

    @pl.when(half_ref[0] != 0)
    def _():
        state = jnp.concatenate([other_ref[...], own_ref[...]], axis=0)
        gain = read_gain(
            other_map_ref[MAP_ROWS : MAP_ROWS + 16, :], other_map_ref[MAP_ROWS + 16 : MAP_ROWS + 32, :]
        )
        state_ref[...] = (
            gain * state
            + dot_nn(state.astype(BF16), other_map_ref[0:DH, :])
            + other_map_ref[DH:MAP_ROWS, :].astype(F32)
        )

    state = state_ref[...]
    for chunk in range(CHUNKS):
        half = state.astype(BF16)
        for step in range(STEPS):
            index = chunk * STEPS + step
            out_ref[index] = (dot_nt(query_part_ref[index], half) + local_ref[index]).astype(BF16)
        if chunk + 1 < CHUNKS:
            changed = sub_map_ref[chunk]
            state = (
                sub_gain_ref[chunk][0:1] * state
                + dot_nn(half, changed[0:DH].astype(BF16))
                + changed[DH:MAP_ROWS]
            )


def mixed_kernel(
    half_ref,
    tok_ref,
    heads_ref,
    residual_ref,
    out_gain_ref,
    ffn_gain_ref,
    mixed_ref,
    send_ref,
    rows_ref,
):
    gain = out_gain_ref[...]
    total = jnp.zeros((TOK, 1), F32)
    for head in range(VALUE_HEADS):
        wide = heads_ref[lax.rem(head + half_ref[0] * 8, VALUE_HEADS)].astype(F32)
        scale = lax.rsqrt(jnp.mean(wide * wide, axis=1, keepdims=True) + 1e-06)
        part = slice(head * DH, head * DH + DH)
        mixed = (residual_ref[:, part].astype(F32) + wide * scale * gain).astype(BF16)
        mixed_ref[:, part] = mixed
        mixed_wide = mixed.astype(F32)
        total = total + jnp.sum(mixed_wide * mixed_wide, axis=1, keepdims=True)
    scale = lax.rsqrt(total * (1.0 / D) + 1e-06)
    swap = swap_matrix()
    for group in range(TOK // 16):
        tokens = slice(group * 16, group * 16 + 16)
        pieces = []
        for c in range(COLS):
            part = slice(c * 128, c * 128 + 128)
            value = mixed_ref[tokens, part].astype(F32) * scale[tokens] * ffn_gain_ref[:, part]
            pieces.append(value.astype(BF16))
        swapped = dot_nn(swap, jnp.concatenate(pieces, axis=0)).astype(BF16)
        rows_ref[tokens] = swapped.reshape(16, 16, 128)

    def place(expert, unused):
        send_ref[2 * expert] = rows_ref[tok_ref[expert]]
        send_ref[2 * expert + 1] = rows_ref[tok_ref[EXPERTS + expert]]
        return unused

    lax.fori_loop(0, EXPERTS, place, 0, unroll=16)


FFN_ROWS = 256


def expert_kernel(rows_ref, gate_ref, up_ref, down_ref, out_ref, wide_ref):
    swap = swap_matrix()
    for pair in range(FFN_ROWS // 32):
        start = pair * 512
        rows = [rows_ref[start : start + 256, :], rows_ref[start + 256 : start + 512, :]]
        tile = dot_nn(swap, jnp.concatenate(rows, axis=1)).astype(BF16)
        for c in range(COLS):
            part = slice(c * 128, c * 128 + 128)
            wide_ref[pair * 32 : pair * 32 + 16, part] = tile[c * 16 : c * 16 + 16, 0:128]
            wide_ref[pair * 32 + 16 : pair * 32 + 32, part] = tile[c * 16 : c * 16 + 16, 128:256]
    wide = wide_ref[...]
    gate = dot_nn(wide, gate_ref[...])
    up = dot_nn(wide, up_ref[...])
    hidden = (gate / (1.0 + jnp.exp(-gate)) * up).astype(BF16)
    wide_ref[...] = dot_nn(hidden, down_ref[...]).astype(BF16)
    for pair in range(FFN_ROWS // 32):
        sides = []
        for start in (pair * 32, pair * 32 + 16):
            pieces = [wide_ref[start : start + 16, c * 128 : c * 128 + 128] for c in range(COLS)]
            sides.append(jnp.concatenate(pieces, axis=0))
        tile = dot_nn(swap, jnp.concatenate(sides, axis=1)).astype(BF16)
        out_ref[pair * 512 : pair * 512 + 256, :] = tile[:, 0:128]
        out_ref[pair * 512 + 256 : pair * 512 + 512, :] = tile[:, 128:256]


def combine_kernel(slot_ref, weight_ref, rows_ref, out_ref, sum_ref):
    def token(index, unused):
        total = jnp.zeros((16, 128), F32)
        for k in range(TOPK):
            place = k * 128 + index
            total = total + weight_ref[place] * rows_ref[slot_ref[place]].astype(F32)
        sum_ref[index] = total.astype(BF16)
        return unused

    lax.fori_loop(0, TOK, token, 0, unroll=4)
    swap = swap_matrix()
    for group in range(TOK // 16):
        tokens = slice(group * 16, group * 16 + 16)
        tile = dot_nn(swap, sum_ref[tokens].reshape(256, 128)).astype(BF16)
        for c in range(COLS):
            out_ref[tokens, c * 128 : c * 128 + 128] = tile[c * 16 : c * 16 + 16]


def shape(dims, dtype):
    return jax.ShapeDtypeStruct(dims, dtype)


SMEM = pl.BlockSpec(memory_space=pltpu.SMEM)
WHOLE = pl.BlockSpec(memory_space=pltpu.VMEM)


def in_hbm(x):
    return pltpu.with_memory_space_constraint(x, pltpu.HBM)


def pack(half, query, key, value, decay, strength):
    return pl.pallas_call(
        pack_kernel,
        out_shape=shape((VALUE_HEADS, PACK_ROWS, 128), BF16),
        in_specs=[SMEM] + [pl.BlockSpec(memory_space=pltpu.HBM)] * 5,
        out_specs=WHOLE,
        scratch_shapes=[
            pltpu.VMEM((VALUE_HEADS, TOK), BF16),
            pltpu.VMEM((VALUE_HEADS, TOK), BF16),
            pltpu.SemaphoreType.DMA((4, VALUE_HEADS)),
        ],
        compiler_params=params(),
        name="pack",
    )(half, *(in_hbm(x) for x in (query, key, value, decay, strength)))


def route(ids, weights):
    return pl.pallas_call(
        route_kernel,
        out_shape=(
            shape((2, EXPERTS), jnp.int32),
            shape((16, 128), jnp.int32),
            shape((16, 128), F32),
        ),
        in_specs=[WHOLE, WHOLE],
        out_specs=(WHOLE, WHOLE, WHOLE),
        compiler_params=params(),
        name="route",
    )(ids, weights)


def mixer(received):
    return pl.pallas_call(
        mixer_kernel,
        out_shape=(
            shape((BLOCKS, BLOCK, DH), BF16),
            shape((BLOCKS, BLOCK, DH), F32),
            shape((CHUNKS, MAP_ROWS, DH), F32),
            shape((CHUNKS, 8, DH), F32),
            shape((HALF_ROWS, DH), BF16),
        ),
        in_specs=[WHOLE],
        out_specs=(WHOLE,) * 5,
        scratch_shapes=[
            pltpu.VMEM((BLOCKS, BLOCK, DH), BF16),
            pltpu.VMEM((BLOCKS, DH, BLOCK), F32),
            pltpu.VMEM((BLOCKS, BLOCK, DH), BF16),
            pltpu.VMEM((BLOCKS, 8, DH), F32),
        ],
        compiler_params=params(),
        name="mixer",
    )(received)


def compose(half, own, other):
    return pl.pallas_call(
        compose_kernel,
        out_shape=shape((SEG_ROWS, DH), BF16),
        in_specs=[SMEM, WHOLE, WHOLE],
        out_specs=WHOLE,
        compiler_params=params(),
        name="compose",
    )(half, own, other)


def fold(position, maps):
    return pl.pallas_call(
        fold_kernel,
        out_shape=shape((WIDTH, DH), F32),
        in_specs=[SMEM, WHOLE],
        out_specs=WHOLE,
        compiler_params=params(),
        name="fold",
    )(position, maps)


def head_rows(half, own, other, other_map, query_part, local, sub_map, sub_gain):
    return pl.pallas_call(
        head_kernel,
        out_shape=shape((BLOCKS, BLOCK, DH), BF16),
        in_specs=[SMEM] + [WHOLE] * 7,
        out_specs=WHOLE,
        scratch_shapes=[pltpu.VMEM((DH, DH), F32)],
        compiler_params=params(),
        name="heads",
    )(half, own, other, other_map, query_part, local, sub_map, sub_gain)


def mix(half, tok, heads, residual, out_gain, ffn_gain):
    return pl.pallas_call(
        mixed_kernel,
        out_shape=(shape((TOK, D), BF16), shape((SLOTS, 16, 128), BF16)),
        in_specs=[SMEM, SMEM] + [WHOLE] * 4,
        out_specs=(WHOLE, WHOLE),
        scratch_shapes=[pltpu.VMEM((TOK, 16, 128), BF16)],
        compiler_params=params(),
        name="mix",
    )(half, tok.reshape(SLOTS), heads, residual, out_gain, ffn_gain)


def experts(rows, gate, up, down):
    hidden = gate.shape[1]
    block = pl.BlockSpec((FFN_ROWS * 16, 128), lambda i: (i, 0))
    return pl.pallas_call(
        expert_kernel,
        grid=(SLOTS // FFN_ROWS,),
        out_shape=shape((SLOTS * 16, 128), BF16),
        in_specs=[
            block,
            pl.BlockSpec((D, hidden), lambda i: (0, 0)),
            pl.BlockSpec((D, hidden), lambda i: (0, 0)),
            pl.BlockSpec((hidden, D), lambda i: (0, 0)),
        ],
        out_specs=block,
        scratch_shapes=[pltpu.VMEM((FFN_ROWS, D), BF16)],
        compiler_params=params(),
        name="experts",
    )(rows, gate, up, down)


def combine(slots, weights, rows):
    return pl.pallas_call(
        combine_kernel,
        out_shape=shape((TOK, D), BF16),
        in_specs=[SMEM, SMEM, WHOLE],
        out_specs=WHOLE,
        scratch_shapes=[pltpu.VMEM((TOK, 16, 128), BF16)],
        compiler_params=params(),
        name="combine",
    )(slots.reshape(16 * 128), weights.reshape(16 * 128), rows)


def swap_all(x, axes):
    return lax.all_to_all(x, axes, split_axis=0, concat_axis=0, tiled=True)


def trade(x):
    return lax.ppermute(x, ("half", "pair"), [(0, 3), (3, 0), (1, 2), (2, 1)])


def body(
    mixer_query,
    mixer_key,
    mixer_value,
    log_decay,
    strength,
    residual,
    out_gain,
    ffn_gain,
    expert_ids,
    expert_weights,
    gate_proj,
    up_proj,
    down_proj,
):
    half = lax.axis_index("half").astype(jnp.int32).reshape(1)
    position = lax.axis_index(EXP_AXES).astype(jnp.int32).reshape(1)
    sent = pack(half, mixer_query[0], mixer_key[0], mixer_value[0], log_decay[0].T, strength[0].T)
    received = swap_all(sent, HEAD_AXES)
    tok, slots, weights = route(expert_ids[0], expert_weights[0])
    query_part, local, sub_map, sub_gain, own_map = mixer(received)
    other_map = trade(own_map)
    maps = lax.all_gather(compose(half, own_map, other_map), EXP_AXES, axis=0)
    own_state = fold(position, maps)
    other_state = trade(own_state)
    outs = head_rows(half, own_state, other_state, other_map, query_part, local, sub_map, sub_gain)
    heads = swap_all(outs, HEAD_AXES)
    mixed, outgoing = mix(
        half, tok, heads, residual[0], out_gain.reshape(1, DH), ffn_gain.reshape(1, D)
    )
    arrived = swap_all(outgoing, ROW_AXES)
    result = experts(arrived.reshape(SLOTS * 16, 128), gate_proj[0], up_proj[0], down_proj[0])
    returned = swap_all(result.reshape(SLOTS, 16, 128), ROW_AXES)
    ffn_out = combine(slots, weights, returned)
    return (mixed[None], ffn_out[None])


def solution(mesh):
    fine = Mesh(mesh.devices.reshape((2,) * 9), OWNER_AXES)
    rows = P(EXP_AXES, SEQ_AXES, None)
    owned = P(OWNER_AXES, None, None)
    return jax.shard_map(
        body,
        mesh=fine,
        in_specs=(rows,) * 6 + (P(), P(), rows, rows) + (owned,) * 3,
        out_specs=(rows, rows),
        check_vma=False,
    )
```
